32 devices in a mesh: rows: 16 (over z, y, x), hid: 2 (over core).
Axes of the slice: x: 2, y: 2, z: 4, core: 2. Of those that a mesh axis runs over, the one named last changes fastest.
Arguments:
- tokens: bfloat16 [16384, 768], P('rows', 'hid'), may hold values from -8 to 8
- teacher: bfloat16 [16384, 768], P('rows', 'hid'), may hold values from -6 to 6
- segment_ids: int32 [32, 512], P('rows'), may hold values from 0 to 3, never falling along the last dimension, each value on 1 to 256 neighbouring positions
- valid_rows: int32 [32, 512], P('rows'), may hold values 0 or 1
- w_query: bfloat16 [768, 768], P(None, 'hid'), may hold values from -0.21875 to 0.21875
- b_query: bfloat16 [768], P('hid'), may hold values from -1.25 to 1.25
- w_key: bfloat16 [768, 768], P(None, 'hid'), may hold values from -0.21875 to 0.21875
- w_value: bfloat16 [768, 768], P(None, 'hid'), may hold values from -0.21875 to 0.21875
- b_value: bfloat16 [768], P('hid'), may hold values from -1.25 to 1.25
- w_out: bfloat16 [768, 768], P('hid'), may hold values from -1.25 to 1.25
- b_out: bfloat16 [768], P('hid'), may hold values from -1.25 to 1.25
- attention_norm_gain: bfloat16 [768], P('hid'), may hold values from 0.5 to 1.5
- first_shift: bfloat16 [768], P('hid'), may hold values from -1.25 to 1.25
- w_up: bfloat16 [768, 3072], P(None, 'hid'), may hold values from -0.21875 to 0.21875
- b_up: bfloat16 [3072], P('hid'), may hold values from -1.25 to 1.25
- w_down: bfloat16 [3072, 768], P('hid'), may hold values from -0.21875 to 0.21875
- b_down: bfloat16 [768], P('hid'), may hold values from -1.25 to 1.25
- feedforward_norm_gain: bfloat16 [768], P('hid'), may hold values from 0.5 to 1.5
- second_shift: bfloat16 [768], P('hid'), may hold values from -1.25 to 1.25
- head_alpha: float32 [12], P('hid'), may hold values from -1 to 3
- head_noise: float32 [12], P('hid'), may hold values from 0.05 to 0.95
- unit_alpha: float32 [3072], P('hid'), may hold values from -1 to 3
- unit_noise: float32 [3072], P('hid'), may hold values from 0.05 to 0.95
- hidden_alpha: float32 [768], P('hid'), may hold values from -1 to 3
- hidden_noise: float32 [768], P('hid'), may hold values from 0.05 to 0.95
- layer_alpha: float32 [2], replicated, may hold values from 0 to 3
- layer_noise: float32 [2], replicated, may hold values from 0.05 to 0.95
- hard_heads: int32 [12], P('hid'), may hold values 0 or 1
- hard_units: int32 [3072], P('hid'), may hold values 0 or 1
- hard_hidden: int32 [768], P('hid'), may hold values 0 or 1
Outputs:
- layer_out: bfloat16 [16384, 768], P('rows', 'hid')
- input_grad: float32 [16384, 768], P('rows', 'hid')
- w_query_grad: float32 [768, 768], P('rows', 'hid')
- b_query_grad: float32 [768], P('hid')
- w_key_grad: float32 [768, 768], P('rows', 'hid')
- w_value_grad: float32 [768, 768], P('rows', 'hid')
- b_value_grad: float32 [768], P('hid')
- w_out_grad: float32 [768, 768], P('hid', 'rows')
- b_out_grad: float32 [768], P('hid')
- first_gain_grad: float32 [768], P('hid')
- first_shift_grad: float32 [768], P('hid')
- w_up_grad: float32 [768, 3072], P('rows', 'hid')
- b_up_grad: float32 [3072], P('hid')
- w_down_grad: float32 [3072, 768], P('hid', 'rows')
- b_down_grad: float32 [768], P('hid')
- second_gain_grad: float32 [768], P('hid')
- second_shift_grad: float32 [768], P('hid')
- head_alpha_grad: float32 [12], P('hid')
- unit_alpha_grad: float32 [3072], P('hid')
- hidden_alpha_grad: float32 [768], P('hid')
- layer_alpha_grad: float32 [2], replicated
- hard_output: bfloat16 [16384, 768], P('rows', 'hid')
- hard_error: float32 [16384], P('rows')
The draws below stay inside these ranges and needn't reach their ends.
Inputs may be any that keep to these rules, and one draw needn't show every extreme that they name: `segment_ids`: within a block the item numbers never fall.
All inputs are finite; a program needn't handle non-finite values. No bound on the sum of `valid_rows` or of `hard_heads` or of `hard_units` or of `hard_hidden` on one device may be relied on, other than what follows from the above.
Results may differ from the reference program's by a relative error of at most 0.015.
Values may be sent and summed in bfloat16 or wider, within the bound.
A program may use at most 128 MiB of HBM per device.

```python
import math
import jax
import jax.numpy as jnp
import numpy as np
from jax import lax

D = 768
HEADS = 12
HEAD = 64
FF = 3072
BLOCK = 512
TOK_DEV = 1024
TOKENS = 16384
BLOCKS = 32


def set_ends(array, own_key, low, top_value):
    index_at = [jax.random.randint(jax.random.fold_in(own_key, axis), (), 0, length) for axis, length in enumerate(array.shape)]
    longest = array.shape.index(max(array.shape))
    next_to = index_at[:longest] + [(index_at[longest] + 1) % array.shape[longest]] + index_at[longest + 1:]
    return array.at[tuple(index_at)].set(low).at[tuple(next_to)].set(top_value)


def with_spikes(array, own_key, source, target, shards_of, factor):
    owner, partner = [(jnp.arange(array.shape[axis_at]) // (array.shape[axis_at] // shards_of)).reshape([-1 if axis == axis_at else 1 for axis in range(array.ndim)]) for axis_at in (source, target)]
    chosen = jax.random.permutation(own_key, shards_of)[partner]
    strong = (owner == chosen) | (owner == (partner + shards_of // 2) % shards_of)
    return jnp.where(strong, factor * array, array)


def levels(rng, dims, pieces, least, high):
    def one(position, blocks):
        steps = jax.random.uniform(jax.random.fold_in(jax.random.fold_in(rng, 6), position), (blocks,), jnp.float32, least / len(pieces), high / len(pieces))
        return jnp.repeat(jnp.exp(steps), dims[position] // blocks).reshape((-1,) + (1,) * (len(dims) - position - 1))

    gain = one(*pieces[0])
    for cut in pieces[1:]:
        gain = gain * one(*cut)
    return gain


def split_up(amount, total, reach, slope):
    weights = [(1 << 20) // math.isqrt(rank ** slope) + 1 for rank in range(2, amount + 1)]
    spare, holding = total - reach - (amount - 1), [1] * (amount - 1)
    while spare > 0:
        movable = [i for i in range(amount - 1) if holding[i] < reach]
        mass, remaining = sum([weights[i] for i in movable]), spare
        for i in movable:
            extra = min(reach - holding[i], max(1, remaining * weights[i] // mass), spare)
            holding[i] = holding[i] + extra
            spare = spare - extra
    return np.array([reach] + holding)


def uneven_parts(rng, count, total, limit, skew):
    if count == 2:
        one = jax.random.randint(rng, (), max(1, total - limit), min(limit, total - 1) + 1)
        return jnp.stack([one, total - one])
    sizes = jnp.asarray(split_up(count, total, limit, skew), jnp.int32)
    pairs = (count - 1) // 2
    giver, sink = sizes[1:1 + 2 * pairs:2], sizes[2:2 + 2 * pairs:2]
    room = jnp.minimum(giver - 1, limit - sink)
    moved = jax.random.randint(jax.random.fold_in(rng, 1), (pairs,), 0, 1 << 20) % (room + 1)
    sizes = sizes.at[1:1 + 2 * pairs:2].set(giver - moved).at[2:2 + 2 * pairs:2].set(sink + moved)
    return sizes[jax.random.permutation(jax.random.fold_in(rng, 2), count)]


def bell_draw(own_key, extent, deviation, limit, pieces=(), held_as=jnp.bfloat16):
    result = deviation * jax.random.normal(own_key, extent, jnp.float32)
    if pieces:
        result = result * levels(own_key, extent, pieces, -0.22, 0.18)
    return jnp.clip(result, -limit, limit).astype(held_as)


def noise_with(stream_key, shape, scale, limit, pieces, heavy, kind=jnp.bfloat16):
    drawn = scale * jax.random.normal(stream_key, shape, jnp.float32)
    if pieces:
        drawn = drawn * levels(stream_key, shape, pieces, -0.22, 0.18)
    return jnp.clip(with_spikes(drawn, jax.random.fold_in(stream_key, 3), *heavy), -limit, limit).astype(kind)


def setup_inputs(seed: int = 0) -> dict:
    streams_of = jax.random.split(jax.random.key(seed), 31)
    return {
        "tokens": noise_with(streams_of[0], (TOKENS, D), 1.0, 8.0, ((0, 16), (1, 2)), (0, 1, 16, 2.0)),
        "teacher": bell_draw(streams_of[1], (TOKENS, D), 1.0, 6.0, ((0, 16), (1, 2))),
        "segment_ids": jax.vmap(lambda own: jnp.searchsorted(jnp.cumsum(uneven_parts(own, 4, BLOCK, BLOCK // 2, 1)), jnp.arange(BLOCK), side="right"))(jax.random.split(streams_of[2], BLOCKS)).reshape((BLOCKS, BLOCK)).astype(jnp.int32),
        "valid_rows": set_ends((jax.random.randint(streams_of[3], (BLOCKS, BLOCK), 0, 8) < 7).astype(jnp.int32), jax.random.fold_in(streams_of[3], 1), 0, 1),
        "w_query": bell_draw(streams_of[4], (D, D), D ** -0.5, 0.21875, ((1, 2),)),
        "b_query": bell_draw(streams_of[5], (D,), 0.2, 1.25, ((0, 2),)),
        "w_key": bell_draw(streams_of[6], (D, D), D ** -0.5, 0.21875, ((1, 2),)),
        "w_value": bell_draw(streams_of[7], (D, D), D ** -0.5, 0.21875, ((1, 2),)),
        "b_value": bell_draw(streams_of[8], (D,), 0.2, 1.25, ((0, 2),)),
        "w_out": bell_draw(streams_of[9], (D, D), (D // 32) ** -0.5, 1.25, ((0, 2),)),
        "b_out": bell_draw(streams_of[10], (D,), 0.2, 1.25, ((0, 2),)),
        "attention_norm_gain": jnp.clip(1.0 + 0.1 * jax.random.normal(streams_of[11], (D,), jnp.float32), 0.5, 1.5).astype(jnp.bfloat16),
        "first_shift": bell_draw(streams_of[12], (D,), 0.2, 1.25, ((0, 2),)),
        "w_up": bell_draw(streams_of[13], (D, FF), D ** -0.5, 0.21875, ((1, 2),)),
        "b_up": bell_draw(streams_of[14], (FF,), 0.2, 1.25, ((0, 2),)),
        "w_down": bell_draw(streams_of[15], (FF, D), (FF // 4) ** -0.5, 0.21875, ((0, 2),)),
        "b_down": bell_draw(streams_of[16], (D,), 0.2, 1.25, ((0, 2),)),
        "feedforward_norm_gain": jnp.clip(1.0 + 0.1 * jax.random.normal(streams_of[17], (D,), jnp.float32), 0.5, 1.5).astype(jnp.bfloat16),
        "second_shift": bell_draw(streams_of[18], (D,), 0.2, 1.25, ((0, 2),)),
        "head_alpha": jnp.clip(-1.0 + 4.0 * jax.random.uniform(streams_of[19], (HEADS,), jnp.float32) ** levels(streams_of[19], (HEADS,), ((0, 2),), -0.2, 0.2), -1.0, 3.0),
        "head_noise": jnp.clip(0.05 + 0.9 * jax.random.uniform(streams_of[20], (HEADS,), jnp.float32) ** levels(streams_of[20], (HEADS,), ((0, 2),), -0.2, 0.2), 0.05, 0.95),
        "unit_alpha": jnp.clip(-1.0 + 4.0 * jax.random.uniform(streams_of[21], (FF,), jnp.float32) ** levels(streams_of[21], (FF,), ((0, 2),), -0.2, 0.2), -1.0, 3.0),
        "unit_noise": jnp.clip(0.05 + 0.9 * jax.random.uniform(streams_of[22], (FF,), jnp.float32) ** levels(streams_of[22], (FF,), ((0, 2),), -0.2, 0.2), 0.05, 0.95),
        "hidden_alpha": jnp.clip(-1.0 + 4.0 * jax.random.uniform(streams_of[23], (D,), jnp.float32) ** levels(streams_of[23], (D,), ((0, 2),), -0.2, 0.2), -1.0, 3.0),
        "hidden_noise": jnp.clip(0.05 + 0.9 * jax.random.uniform(streams_of[24], (D,), jnp.float32) ** levels(streams_of[24], (D,), ((0, 2),), -0.2, 0.2), 0.05, 0.95),
        "layer_alpha": jnp.clip(jax.random.uniform(streams_of[25], (2,), jnp.float32, 0.0, 3.0), 0.0, 3.0),
        "layer_noise": jnp.clip(jax.random.uniform(streams_of[26], (2,), jnp.float32, 0.05, 0.95), 0.05, 0.95),
        "hard_heads": set_ends((jax.random.randint(streams_of[27], (HEADS,), 0, 4) < 3).astype(jnp.int32), jax.random.fold_in(streams_of[27], 1), 0, 1),
        "hard_units": set_ends((jax.random.randint(streams_of[28], (FF,), 0, 4) < 3).astype(jnp.int32), jax.random.fold_in(streams_of[28], 1), 0, 1),
        "hard_hidden": set_ends((jax.random.randint(streams_of[29], (D,), 0, 4) < 3).astype(jnp.int32), jax.random.fold_in(streams_of[29], 1), 0, 1),
    }


@jax.custom_vjp
def low(v):
    return lax.optimization_barrier(v.astype(jnp.bfloat16)).astype(jnp.float32)

@jax.custom_vjp
def low_back(v):
    return v

def low_keep(v):
    return (low(v), None)

def low_pass(kept, incoming_gradient):
    return (incoming_gradient,)

def back_keep(v):
    return (v, None)

def back_low(kept, incoming_gradient):
    return (low(incoming_gradient),)
low.defvjp(low_keep, low_pass)
low_back.defvjp(back_keep, back_low)
highest = lax.Precision.HIGHEST
temper = 2.0 / 3.0
norm_eps = 1e-12
masked_score = -1e+30

def gate_value(alpha, noise):
    return jax.nn.sigmoid((jnp.log(noise) - jnp.log(1.0 - noise) + alpha) / temper)

def product(left, right):
    return jnp.dot(left, right, precision=highest, preferred_element_type=jnp.float32)

def normalize(residual_state, norm_gain_value, norm_shift_value, retained_mask):
    average_value = lax.optimization_barrier(jnp.mean(residual_state, -1, keepdims=True))
    variance = lax.optimization_barrier(jnp.mean(residual_state * residual_state, -1, keepdims=True)) - average_value * average_value
    return ((residual_state - average_value) * lax.rsqrt(variance + norm_eps) * norm_gain_value + norm_shift_value) * retained_mask

def attend_block(query, keyed, value, segments, valid):
    scores = jnp.einsum('qhd,khd->hqk', query, keyed, precision=highest) * HEAD ** (-0.5)
    scores = low_back(scores)
    positions = jnp.arange(BLOCK)
    allowed = (segments[:, None] == segments[None, :]) & (valid[None, :] > 0)
    allowed = allowed | (positions[:, None] == positions[None, :])
    scores = jnp.where(allowed[None], scores, masked_score)
    weights = jax.nn.softmax(scores, axis=-1)
    return jnp.einsum('hqk,khd->qhd', low(weights), value, precision=highest)

def layer(params, gates, inputs, segments, valid):
    w_query, b_query, w_key, w_value, b_value, w_out, b_out, attention_norm_gain, first_shift, w_up, b_up, w_down, b_down, feedforward_norm_gain, second_shift = params
    z_head, z_unit, z_hidden, z_attn, z_ffn = gates
    row_count = inputs.shape[0]
    query = low(low_back(product(inputs, w_query) + b_query))
    keyed = low(low_back(product(inputs, w_key)))
    value = low(low_back(product(inputs, w_value) + b_value))
    shaped = (row_count // BLOCK, BLOCK, HEADS, HEAD)
    checked = jax.checkpoint(attend_block)
    context = lax.map(lambda parts: checked(parts[0], parts[1], parts[2], parts[3], parts[4]), (query.reshape(shaped), keyed.reshape(shaped), value.reshape(shaped), segments, valid))
    context = low_back(context.reshape(row_count, HEADS, HEAD))
    mixed = low(context * z_head[None, :, None]).reshape(row_count, D)
    branch = low_back(product(mixed, w_out))
    residual_state = inputs + z_attn * branch + b_out
    hidden_state = normalize(residual_state, attention_norm_gain, first_shift, z_hidden)
    upper = low_back(product(low(hidden_state), w_up) + b_up)
    active = low(jax.nn.gelu(upper, approximate=True) * z_unit)
    down = low_back(product(active, w_down))
    resid_second = hidden_state + z_ffn * down + b_down
    return normalize(resid_second, feedforward_norm_gain, second_shift, z_hidden)

def reference(tokens, teacher, segment_ids, valid_rows, w_query, b_query, w_key, w_value, b_value, w_out, b_out, attention_norm_gain, first_shift, w_up, b_up, w_down, b_down, feedforward_norm_gain, second_shift, head_alpha, head_noise, unit_alpha, unit_noise, hidden_alpha, hidden_noise, layer_alpha, layer_noise, hard_heads, hard_units, hard_hidden):
    params = tuple((item.astype(jnp.float32) for item in (w_query, b_query, w_key, w_value, b_value, w_out, b_out, attention_norm_gain, first_shift, w_up, b_up, w_down, b_down, feedforward_norm_gain, second_shift)))
    alphas = (head_alpha, unit_alpha, hidden_alpha, layer_alpha)
    one_value = jnp.ones((), jnp.float32)
    hard_gates = (hard_heads.astype(jnp.float32), hard_units.astype(jnp.float32), hard_hidden.astype(jnp.float32), one_value, one_value)
    group = TOK_DEV // BLOCK
    visits = BLOCKS // group
    sliced = (tokens.reshape(visits, group * BLOCK, D), teacher.reshape(visits, group * BLOCK, D), segment_ids.reshape(visits, group, BLOCK), valid_rows.reshape(visits, group, BLOCK))

    def soft_gates(alpha_set):
        head_a, unit_a, hidden_a, layer_a = alpha_set
        return (gate_value(head_a, head_noise), gate_value(unit_a, unit_noise), gate_value(hidden_a, hidden_noise), gate_value(layer_a[0], layer_noise[0]), gate_value(layer_a[1], layer_noise[1]))

    def visit(totals, parts):
        token_rows, teacher_rows, segments, valid = parts
        inputs = token_rows.astype(jnp.float32)
        target = teacher_rows.astype(jnp.float32)

        def forward(param_set, alpha_set, rows_in):
            return layer(param_set, soft_gates(alpha_set), rows_in, segments, valid)
        final_output, pull = jax.vjp(forward, params, alphas, inputs)
        retained_mask = valid.reshape(-1, 1).astype(jnp.float32)
        grad_params, grad_alphas, grad_inputs = pull(retained_mask * (final_output - target))
        hard_final = layer(params, hard_gates, inputs, segments, valid)
        error = lax.optimization_barrier(jnp.mean((hard_final - target) * (hard_final - target), -1))
        totals = jax.tree.map(jnp.add, totals, (grad_params, grad_alphas))
        return (totals, (final_output.astype(jnp.bfloat16), grad_inputs, hard_final.astype(jnp.bfloat16), error))
    start = jax.tree.map(jnp.zeros_like, (params, alphas))
    (grad_params, grad_alphas), stacked = lax.scan(visit, start, sliced)
    layer_out = stacked[0].reshape(TOKENS, D)
    input_grad = stacked[1].reshape(TOKENS, D)
    hard_output = stacked[2].reshape(TOKENS, D)
    hard_error = stacked[3].reshape(TOKENS)
    return (layer_out, input_grad, grad_params[0], grad_params[1], grad_params[2], grad_params[3], grad_params[4], grad_params[5], grad_params[6], grad_params[7], grad_params[8], grad_params[9], grad_params[10], grad_params[11], grad_params[12], grad_params[13], grad_params[14], grad_alphas[0], grad_alphas[1], grad_alphas[2], grad_alphas[3], hard_output, hard_error)
```

```python
import functools

import jax
import jax.numpy as jnp
from jax import lax
from jax.experimental import pallas as pl
from jax.experimental.pallas import tpu as pltpu
from jax.sharding import PartitionSpec as P

HEAD = 64
f32 = jnp.float32
bf16 = jnp.bfloat16
MESH = pl.DeviceIdType.MESH

temper = 2.0 / 3.0
norm_eps = 1e-12
masked_score = -1e30

PB_Q, PB_V, PB_O, PG1, PS1, PB_D, PG2, PS2, PZH, PHH, PZHEAD, PHHEAD, PZA, PZF = range(14)
S_BQ, S_BV, S_BO, S_G1, S_S1, S_BD, S_G2, S_S2, S_ZH, S_ZHEAD, S_ZA, S_ZF = range(12)
X_TOK, X_HID, X_DDOWN = range(3)
X_DBR = X_DDOWN


def gate_value(alpha, noise):
    return jax.nn.sigmoid((jnp.log(noise) - jnp.log(1.0 - noise) + alpha) / temper)


def mm(a, b):
    return lax.dot_general(a, b, (((1,), (0,)), ((), ())), preferred_element_type=f32)


def mm_nt(a, b):
    return lax.dot_general(a, b, (((1,), (1,)), ((), ())), preferred_element_type=f32)


def loop(count, body):
    def step(i, carry):
        body(i)
        return carry

    lax.fori_loop(0, count, step, 0)


def al(x, m):
    return pl.multiple_of(x, m)


def layer_kernel(dims, *refs):
    n, D, F, M, use_rs = dims
    DH, FH = D // 2, F // 2
    heads = D // HEAD
    pairs = heads // 2
    groups = 4 + 2 * (FH // DH)
    fgroups = FH // DH
    (
        tok_h,
        tea_h,
        seg_ref,
        valid_ref,
        wq_h,
        wk_h,
        wv_h,
        wout_h,
        wup_h,
        wdown_h,
        pd_h,
        pf_h,
    ) = refs[:12]
    count = 8 if use_rs else 6
    outs = refs[12 : 12 + count]
    layer_out_h, input_grad_h, hard_out_h, err_out, vec_out = outs[:5]
    (
        tok,
        tea,
        wqkv,
        wout,
        wup,
        wdown,
        pd,
        pf,
        qkv,
        qkv_peer,
        bias,
        probs,
        ctx,
        mixed,
        mixed_peer,
        resid,
        hbf,
        acc,
        act,
        act_peer,
        gp,
        dup_peer,
        dres,
        dbf,
        xt,
        vd,
        vf,
        pack,
        packr,
        packs,
        errs,
        G,
        recv1,
        recv2,
        recv3,
        lsem,
        ssem,
        rsem,
        xs,
        xr,
        s1,
        r1,
        s2,
        r2,
        s3,
        r3,
        credit,
    ) = refs[12 + count :]

    r = lax.axis_index("rows")
    h = lax.axis_index("hid")
    oh = 1 - h
    peer = (r, oh)
    x = lax.rem(r, 2)
    y = lax.rem(lax.div(r, 2), 2)
    z = lax.div(r, 4)
    zc = n // 4

    def chip(cx, cy, cz):
        return (cz * 4 + cy * 2 + cx, h)

    barrier = pltpu.get_barrier_semaphore()
    partners = [peer]
    if use_rs:
        partners += [chip(1 - x, y, z), chip(x, 1 - y, z), chip(1 - x, 1 - y, z)]
        partners += [chip(x, y, lax.rem(z + d, zc)) for d in range(1, zc)]
    for p in partners:
        pl.semaphore_signal(barrier, inc=1, device_id=p, device_id_type=MESH)
    pl.semaphore_wait(barrier, len(partners))

    cols = pl.ds(al(h * DH, 128), DH)
    ocols = pl.ds(al(oh * DH, 128), DH)
    fcols = pl.ds(al(h * FH, 128), FH)
    ofcols = pl.ds(al(oh * FH, 128), FH)
    mine = pl.ds(al(h * M, 128), M)
    other = pl.ds(al(oh * M, 128), M)
    feeds = [
        (pd_h, pd_h, pd.at[:, cols]),
        (pf_h, pf_h, pf.at[:, fcols]),
        (tok_h.at[mine], tok_h.at[other], tok.at[:, cols]),
        (wq_h, wq_h, wqkv.at[:, pl.ds(al(h * DH, 128), DH)]),
        (wk_h, wk_h, wqkv.at[:, pl.ds(al(h * DH + D, 128), DH)]),
        (wv_h, wv_h, wqkv.at[:, pl.ds(al(h * DH + 2 * D, 128), DH)]),
        (wout_h, wout_h, wout.at[cols]),
        (wup_h, wup_h, wup.at[:, fcols]),
        (wdown_h, wdown_h, wdown.at[fcols]),
        (tea_h.at[mine], tea_h.at[other], tea.at[:, cols]),
    ]
    local = []
    remote = []
    for i, (src, src_other, dst) in enumerate(feeds):
        far = pltpu.make_async_remote_copy(
            src_ref=src_other,
            dst_ref=dst,
            send_sem=ssem.at[i],
            recv_sem=rsem.at[i],
            device_id=peer,
            device_id_type=MESH,
        )
        far.start()
        near = pltpu.make_async_copy(src, dst, lsem.at[i])
        near.start()
        local.append(near)
        remote.append(far)

    def fed(*which):
        for i in which:
            local[i].wait()
            remote[i].wait_recv()

    def to_peer(k, src, dst):
        copy = pltpu.make_async_remote_copy(
            src_ref=src,
            dst_ref=dst,
            send_sem=xs.at[k],
            recv_sem=xr.at[k],
            device_id=peer,
            device_id_type=MESH,
        )
        copy.start()
        return copy

    def far_copy(src, dst, send, recv, device):
        return pltpu.make_async_remote_copy(
            src_ref=src,
            dst_ref=dst,
            send_sem=send,
            recv_sem=recv,
            device_id=device,
            device_id_type=MESH,
        )

    def send1(g, first):
        if first == 0:
            return far_copy(G.at[g, :, :, 1 - x], recv1.at[g], s1.at[g], r1.at[g], chip(1 - x, y, z))
        return far_copy(G.at[g, :, 1 - y], recv1.at[g], s1.at[g], r1.at[g], chip(x, 1 - y, z))

    def send2(g, first):
        if first == 0:
            return far_copy(
                G.at[g, :, 1 - y, x], recv2.at[g], s2.at[g], r2.at[g], chip(x, 1 - y, z)
            )
        return far_copy(G.at[g, :, y, 1 - x], recv2.at[g], s2.at[g], r2.at[g], chip(1 - x, y, z))

    def send3(g, d):
        to = lax.rem(z + d, zc)
        return far_copy(
            G.at[g, to, y, x], recv3.at[g, d - 1], s3.at[g, d - 1], r3.at[g, d - 1], chip(x, y, to)
        )

    def stage1(g, first):
        send1(g, first).wait_recv()

        def body(k):
            for j in range(2):
                if first == 0:
                    at = G.at[g, k, j, x]
                else:
                    at = G.at[g, k, y, j]
                at[...] = (at[...].astype(f32) + recv1[g, k, j].astype(f32)).astype(bf16)

        loop(zc, body)
        send2(g, first).start()

    def stage2(g, first):
        send2(g, first).wait_recv()

        def body(k):
            at = G.at[g, k, y, x]
            at[...] = (at[...].astype(f32) + recv2[g, k].astype(f32)).astype(bf16)

        loop(zc, body)
        for d in range(1, zc):
            send3(g, d).start()

    def final(g):
        for d in range(1, zc):
            send3(g, d).wait_recv()
        total = G[g, z, y, x].astype(f32)
        for d in range(1, zc):
            total = total + recv3[g, d - 1].astype(f32)
        return total

    npairs = groups // 2

    def tick(i):
        if not use_rs:
            return

        @pl.when(i < npairs)
        def _():
            for b in range(2):
                stage1(2 * i + b, b)

        @pl.when((i >= 1) & (i < npairs + 1))
        def _():
            for b in range(2):
                stage2(2 * i - 2 + b, b)

    RT = 64

    def row_loop(body):
        loop(M // RT, lambda i: body(pl.ds(al(i * RT, RT), RT)))

    def add_sum(k, value):
        at = vd.at[pl.ds(8 * k, 8)]
        at[...] = at[...] + jnp.sum(value.reshape(RT // 8, 8, D), axis=0)

    def par(k):
        return pd[pl.ds(k, 1), :]

    def normed(resid_tile):
        mean = jnp.sum(resid_tile, -1, keepdims=True) / D
        var = jnp.sum(resid_tile * resid_tile, -1, keepdims=True) / D - mean * mean
        inv = lax.rsqrt(var + norm_eps)
        return (resid_tile - mean) * inv, inv

    dctx = outb = hbf

    def transpose_to(src, k, sem):
        def body(i):
            at = pl.ds(al(i * 128, 128), 128)
            xt[k, :, at] = src[at, :].T

        loop(M // 128, body)
        return to_peer(sem, xt.at[k, :, pl.ds(0, M)], xt.at[k, :, pl.ds(M, M)])

    NT = 256

    def tiles(count, body):
        loop(count // NT, lambda i: body(pl.ds(al(i * NT, NT), NT)))

    def project_out(gate):
        def body(at):
            acc[:, at] = mm(mixed[...], wout[:, at])

        tiles(D, body)

        def rows_body(at):
            value = tok[at, :].astype(f32) + acc[at, :] * gate + par(PB_O)
            resid[at, :] = value

        row_loop(rows_body)

    def first_norm(mask):
        def body(at):
            xh, inv = normed(resid[at, :])
            hbf[at, :] = ((xh * par(PG1) + par(PS1)) * par(mask)).astype(bf16)

        row_loop(body)

    def up(unit_row, keep):
        def body(at):
            u = mm(hbf[...], wup[:, at]) + pf[pl.ds(0, 1), at]
            u2 = u * u
            half = 0.5 * jnp.tanh(u * (0.7978845608 + (0.7978845608 * 0.044715) * u2)) + 0.5
            act[:, at] = (u * half * pf[pl.ds(unit_row, 1), at]).astype(bf16)
            if keep:
                slope = half + u * (2.0 * half * (1.0 - half)) * (
                    0.7978845608 + (3.0 * 0.7978845608 * 0.044715) * u2
                )
                gp[:, at] = slope.astype(bf16)

        tiles(F, body)

    def down():
        def body(at):
            acc[:, at] = mm(act[...], wdown[:, at])

        tiles(D, body)

    row_seg = seg_ref[pl.ds(h, 1), :].astype(f32)
    row_valid = valid_ref[pl.ds(h, 1), :].astype(f32)
    col_seg = jnp.broadcast_to(row_seg, (128, M)).T[:, :1]
    col_valid = jnp.broadcast_to(row_valid, (128, M)).T
    errs[...] = jnp.zeros_like(errs)
    vd[...] = jnp.zeros_like(vd)
    diagonal = lax.broadcasted_iota(jnp.int32, (M, M), 0) == lax.broadcasted_iota(
        jnp.int32, (M, M), 1
    )
    allowed = ((col_seg == row_seg) & (row_valid > 0)) | diagonal
    bias[...] = jnp.where(allowed, 0.0, masked_score).astype(bf16)
    keep_ref = errs
    keep_ref[...] = col_valid

    fed(0, 1, 2, 3, 4, 5)

    for part, row in ((0, PB_Q), (1, None), (2, PB_V)):

        def body(i, part=part, row=row):
            at = pl.ds(al(i * NT, NT), NT)
            wide = pl.ds(al(i * NT + part * D, NT), NT)
            value = mm(tok[...], wqkv[:, wide])
            if row is not None:
                value = value + pd[pl.ds(row, 1), at]
            value = value.astype(bf16)
            if part == 0:
                value = value * jnp.asarray(HEAD**-0.5, bf16)
            qkv[:, wide] = value

        loop(D // NT, body)

    tok_copy = transpose_to(tok, X_TOK, 0)

    lane = lax.broadcasted_iota(jnp.int32, (1, 2 * HEAD), 1)
    head_mask = [(lane < HEAD).astype(bf16), (lane >= HEAD).astype(bf16)]

    QT = 256

    def attend(i):
        p = lax.div(i, M // QT)
        rows = pl.ds(al(lax.rem(i, M // QT) * QT, QT), QT)
        at = pl.ds(al(p * 128, 128), 128)
        q2 = qkv[rows, at]
        k2 = qkv[:, pl.ds(al(p * 128 + D, 128), 128)]
        v2 = qkv[:, pl.ds(al(p * 128 + 2 * D, 128), 128)]
        total = None
        for b in range(2):
            s = mm_nt(q2 * head_mask[b], k2) + bias[rows, :].astype(f32)
            e = jnp.exp(s - jnp.max(s, -1, keepdims=True))
            w = (e * (1.0 / jnp.sum(e, -1, keepdims=True))).astype(bf16)
            probs[2 * p + b, rows] = w
            part = mm(w, v2 * head_mask[b])
            total = part if total is None else total + part
        ctx[rows, at] = total.astype(bf16)
        mixed[rows, at] = (total * pd[pl.ds(PZHEAD, 1), at]).astype(bf16)

    loop(pairs * (M // QT), attend)
    mixed_copy = to_peer(4, mixed.at[:, ocols], mixed_peer)

    fed(6)
    project_out(par(PZA))
    first_norm(PZH)
    hid_copy = transpose_to(hbf, X_HID, 1)
    fed(7)
    up(1, True)
    act_copy = to_peer(5, act.at[:, ofcols], act_peer)
    fed(8, 9)
    down()

    def second_norm(at):
        xh1, inv1 = normed(resid[at, :])
        hidden = (xh1 * par(PG1) + par(PS1)) * par(PZH)
        dn = acc[at, :]
        xh, inv = normed(hidden + par(PZF) * dn + par(PB_D))
        nrm = xh * par(PG2) + par(PS2)
        fin = nrm * par(PZH)
        outb[at, :] = fin.astype(bf16)
        d = keep_ref[at, :][:, :1] * (fin - tea[at, :].astype(f32))
        dz = d * par(PZH)
        add_sum(S_S2, dz)
        add_sum(S_G2, dz * xh)
        add_sum(S_ZH, d * nrm)
        e = dz * par(PG2)
        dr = inv * (
            e - jnp.sum(e, -1, keepdims=True) / D - xh * (jnp.sum(e * xh, -1, keepdims=True) / D)
        )
        add_sum(S_BD, dr)
        add_sum(S_ZF, dr * dn)
        dres[at, :] = dr
        dbf[at, :] = (dr * par(PZF)).astype(bf16)

    row_loop(second_norm)
    out_near = pltpu.make_async_copy(outb.at[:, cols], layer_out_h.at[mine], lsem.at[10])
    out_near.start()
    out_far = to_peer(6, outb.at[:, ocols], layer_out_h.at[mine])

    ddown_copy = transpose_to(dbf, X_DDOWN, 2)

    def dactive_tile(at):
        da = mm_nt(dbf[...], wdown[at, :])
        su = jnp.sum((da * act[:, at].astype(f32)).reshape(M // 8, 8, NT), axis=0)
        vf[pl.ds(8, 8), at] = su
        du = (da * pf[pl.ds(1, 1), at] * gp[:, at].astype(f32)).astype(bf16)
        gp[:, at] = du
        vf[pl.ds(0, 8), at] = jnp.sum(du.astype(f32).reshape(M // 8, 8, NT), axis=0)

    tiles(F, dactive_tile)
    dup_copy = to_peer(7, gp.at[:, ofcols], dup_peer)

    GT = D // 4

    def grad_group(g, k, own, own_at, far, far_at):
        def body(i):
            at = pl.ds(al(i * GT, GT), GT)
            value = mm(xt[k, at, pl.ds(0, M)], own[:, own_at]) + mm(
                xt[k, at, pl.ds(M, M)], far[:, far_at]
            )
            if use_rs:
                G[g, i] = value.astype(bf16).reshape(2, 2, D // n, DH)
            else:
                G[g, at] = value.astype(bf16)

        loop(4, body)

    def start1(g, first):
        if use_rs:
            send1(g, first).start()

    ddown_copy.wait_recv()
    act_copy.wait_recv()

    def down_grad(i):
        for b in range(2):
            g = 2 * i + b
            grad_group(
                g,
                X_DDOWN,
                act,
                pl.ds(al(h * FH + g * DH, 128), DH),
                act_peer,
                pl.ds(al(g * DH, 128), DH),
            )
            start1(g, b)

    loop(fgroups // 2, down_grad)
    pl.semaphore_signal(credit, inc=1, device_id=peer, device_id_type=MESH)

    def dhidden_tile(at):
        acc[:, at] = mm_nt(gp[...], wup[at, :])

    tiles(D, dhidden_tile)

    hid_copy.wait_recv()
    dup_copy.wait_recv()

    def up_grad(i):
        for b in range(2):
            g = 2 * i + b
            grad_group(
                g + fgroups,
                X_HID,
                gp,
                pl.ds(al(h * FH + g * DH, 128), DH),
                dup_peer,
                pl.ds(al(g * DH, 128), DH),
            )
            start1(g + fgroups, b)

    loop(fgroups // 2, up_grad)

    def first_norm_back(at):
        value = resid[at, :]
        xh, inv = normed(value)
        dh = dres[at, :] + acc[at, :]
        dz = dh * par(PZH)
        add_sum(S_S1, dz)
        add_sum(S_G1, dz * xh)
        add_sum(S_ZH, dh * (xh * par(PG1) + par(PS1)))
        e = dz * par(PG1)
        dr = inv * (
            e - jnp.sum(e, -1, keepdims=True) / D - xh * (jnp.sum(e * xh, -1, keepdims=True) / D)
        )
        add_sum(S_BO, dr)
        add_sum(S_ZA, dr * (value - tok[at, :].astype(f32) - par(PB_O)))
        dres[at, :] = dr
        dbf[at, :] = (dr * par(PZA)).astype(bf16)

    row_loop(first_norm_back)
    tick(0)
    out_near.wait()
    out_far.wait_send()
    ddown_copy.wait_send()
    pl.semaphore_wait(credit, 1)
    dbr_copy = transpose_to(dbf, X_DBR, 3)

    def dmixed_tile(at):
        dm = mm_nt(dbf[...], wout[at, :])
        vd[pl.ds(8 * S_ZHEAD, 8), at] = jnp.sum(
            (dm * ctx[:, at].astype(f32)).reshape(M // 8, 8, NT), axis=0
        )
        dctx[:, at] = (dm * pd[pl.ds(PZHEAD, 1), at]).astype(bf16)

    tiles(D, dmixed_tile)
    dbr_copy.wait_recv()
    mixed_copy.wait_recv()
    g_out = 2 * fgroups
    grad_group(g_out, X_DBR, mixed, cols, mixed_peer, pl.ds(0, DH))
    start1(g_out, 0)

    qkv_copies = [
        far_copy(
            qkv.at[:, pl.ds(al(oh * DH + j * D, 128), DH)],
            qkv_peer.at[:, pl.ds(j * DH, DH)],
            xs.at[9 + j],
            xr.at[9 + j],
            peer,
        )
        for j in range(3)
    ]
    scale = HEAD**-0.5

    def attend_back(i):
        p = lax.rem(oh * (pairs // 2) + i, pairs)
        qa = pl.ds(al(p * 128, 128), 128)
        ka = pl.ds(al(p * 128 + D, 128), 128)
        va = pl.ds(al(p * 128 + 2 * D, 128), 128)
        k2, v2 = qkv[:, ka], qkv[:, va]
        dkt = dvt = None
        parts = []
        for t in range(M // QT):
            rows = pl.ds(t * QT, QT)
            q2, c2 = qkv[rows, qa], dctx[rows, qa]
            dq = None
            for b in range(2):
                m = head_mask[b]
                w = probs[2 * p + b, rows]
                wf = w.astype(f32)
                dp = mm_nt(c2 * m, v2)
                delta = jnp.sum(wf * dp, -1, keepdims=True)
                ds = (wf * (dp - delta)).astype(bf16)
                a = mm(ds, k2 * m)
                bb = mm((q2 * m).T, ds)
                c = mm((c2 * m).T, w)
                dq = a if dq is None else dq + a
                dkt = bb if dkt is None else dkt + bb
                dvt = c if dvt is None else dvt + c
            parts.append((dq * scale).astype(bf16))
        dq = jnp.concatenate(parts, axis=0)
        dk = dkt.astype(bf16).T
        dv = dvt.astype(bf16).T
        qkv[:, qa] = dq
        qkv[:, ka] = dk
        qkv[:, va] = dv
        vd[pl.ds(8 * S_BQ, 8), qa] = jnp.sum(dq.astype(f32).reshape(M // 8, 8, 128), axis=0)
        vd[pl.ds(8 * S_BV, 8), qa] = jnp.sum(dv.astype(f32).reshape(M // 8, 8, 128), axis=0)

        @pl.when(i == pairs // 2 - 1)
        def _():
            for copy in qkv_copies:
                copy.start()

        @pl.when(lax.rem(i, 2) == 1)
        def _():
            tick(1 + lax.div(i, 2))

    loop(pairs, attend_back)
    tok_copy.wait_recv()
    for copy in qkv_copies:
        copy.wait_recv()

    for j in range(3):
        g = g_out + 1 + j
        grad_group(
            g,
            X_TOK,
            qkv,
            pl.ds(al(h * DH + j * D, 128), DH),
            qkv_peer,
            pl.ds(j * DH, DH),
        )
        start1(g, (1 + j) % 2)

    sums = jnp.sum(vd[...].reshape(16, 8, D), axis=1)
    fsums = jnp.sum(vf[...].reshape(2, 8, F), axis=1)
    fold = sums[S_ZA : S_ZF + 1, :DH] + sums[S_ZA : S_ZF + 1, DH:]
    for c in range(2):
        pack[c, 0:16, :] = sums[:, c * DH : (c + 1) * DH]
        pack[c, S_ZA : S_ZF + 1, :] = fold
        for j in range(fgroups):
            pack[c, 16 + 2 * j : 18 + 2 * j, :] = fsums[:, c * FH + j * DH : c * FH + (j + 1) * DH]
    pack_copy = to_peer(8, pack.at[oh], packr)

    def input_tile(at):
        acc[:, at] = dres[:, at] + mm_nt(qkv[...], wqkv[at, :])

    tiles(D, input_tile)
    in_near = pltpu.make_async_copy(acc.at[:, cols], input_grad_h.at[mine], lsem.at[11])
    in_near.start()
    in_far = far_copy(acc.at[:, ocols], input_grad_h.at[mine], xs.at[12], xr.at[12], peer)
    in_far.start()

    pack_copy.wait_recv()
    packs[0] = pack[h] + packr[...]
    plane = []
    if use_rs:
        for k, (cx, cy) in enumerate(((1 - x, y), (x, 1 - y), (1 - x, 1 - y))):
            copy = far_copy(packs.at[0], packs.at[1 + k], xs.at[13 + k], xr.at[13 + k], chip(cx, cy, z))
            copy.start()
            plane.append(copy)
    tick(4)

    in_near.wait()
    in_far.wait_send()
    mixed_copy.wait_send()
    mixed[...] = (ctx[...].astype(f32) * par(PHHEAD)).astype(bf16)
    project_out(1.0)
    first_norm(PHH)
    act_copy.wait_send()
    tick(5)
    zsum = []
    if use_rs:
        for copy in plane:
            copy.wait_recv()
        packs[4] = (packs[0] + packs[1]) + (packs[2] + packs[3])
        for d in range(1, zc):
            to = lax.rem(z + d, zc)
            copy = far_copy(
                packs.at[4], packs.at[4 + d], xs.at[17 + d], xr.at[17 + d], chip(x, y, to)
            )
            copy.start()
            zsum.append(copy)
    up(2, False)
    tick(6)
    down()

    def hard_norm(at):
        xh1, inv1 = normed(resid[at, :])
        hidden = (xh1 * par(PG1) + par(PS1)) * par(PHH)
        xh, inv = normed(hidden + acc[at, :] + par(PB_D))
        fin = (xh * par(PG2) + par(PS2)) * par(PHH)
        outb[at, :] = fin.astype(bf16)
        diff = fin - tea[at, :].astype(f32)
        err = jnp.sum(diff * diff, -1, keepdims=True) / D
        keep_ref[at, :] = jnp.broadcast_to(err, (RT, 128))

    row_loop(hard_norm)
    hard_near = pltpu.make_async_copy(outb.at[:, cols], hard_out_h.at[mine], lsem.at[12])
    hard_near.start()
    hard_far = far_copy(outb.at[:, ocols], hard_out_h.at[mine], xs.at[16], xr.at[16], peer)
    hard_far.start()
    pack_copy.wait_send()
    recv_err = vf.at[pl.ds(0, 8), pl.ds(0, M)]
    send_err = vf.at[pl.ds(8, 8), pl.ds(0, M)]
    send_err[...] = errs[...].T[0:8, :]
    err_copy = far_copy(send_err, recv_err, xs.at[17], xr.at[17], peer)
    err_copy.start()

    if use_rs:
        attn_grad_out, up_grad_out, down_grad_out = outs[5:]
        pr = D // n
        grads = []
        for g in range(groups):
            at = acc.at[pl.ds((g // 2) * pr, pr), pl.ds((g % 2) * DH, DH)]
            at[...] = final(g)
            if g < fgroups:
                to = down_grad_out.at[:, pl.ds(g * DH, DH)]
            elif g < 2 * fgroups:
                to = up_grad_out.at[:, pl.ds((g - fgroups) * DH, DH)]
            else:
                to = attn_grad_out.at[g - 2 * fgroups]
            copy = pltpu.make_async_copy(at, to, lsem.at[13 + g])
            copy.start()
            grads.append(copy)
        for copy in zsum:
            copy.wait_recv()
        total = packs[4]
        for d in range(1, zc):
            total = total + packs[4 + d]
        vec_out[...] = total
    else:
        vec_out[...] = packs[0]
        grads_near = pltpu.make_async_copy(G, outs[5], lsem.at[13])
        grads_near.start()
        grads_near.wait()
    err_copy.wait_recv()
    err_out[pl.ds(h, 1), :] = send_err[0:1, :]
    err_out[pl.ds(oh, 1), :] = recv_err[0:1, :]

    hard_near.wait()
    hard_far.wait()
    in_far.wait_recv()
    out_far.wait_recv()
    err_copy.wait_send()
    for copy in remote:
        copy.wait_send()
    tok_copy.wait_send()
    hid_copy.wait_send()
    dbr_copy.wait_send()
    dup_copy.wait_send()
    for copy in qkv_copies:
        copy.wait_send()
    if use_rs:
        for copy in grads:
            copy.wait()
        for copy in plane + zsum:
            copy.wait_send()
        for g in range(groups):
            send1(g, g % 2).wait_send()
            send2(g, g % 2).wait_send()
            for d in range(1, zc):
                send3(g, d).wait_send()


def shards(rows, *args):
    (
        tokens,
        teacher,
        segment_ids,
        valid_rows,
        w_query,
        b_query,
        w_key,
        w_value,
        b_value,
        w_out,
        b_out,
        attention_norm_gain,
        first_shift,
        w_up,
        b_up,
        w_down,
        b_down,
        feedforward_norm_gain,
        second_shift,
        head_alpha,
        head_noise,
        unit_alpha,
        unit_noise,
        hidden_alpha,
        hidden_noise,
        layer_alpha,
        layer_noise,
        hard_heads,
        hard_units,
        hard_hidden,
    ) = args
    DH = tokens.shape[1]
    D = w_query.shape[0]
    FH = w_up.shape[1]
    F = 2 * FH
    blocks, M = segment_ids.shape
    n = rows
    use_rs = n % 4 == 0 and D % n == 0 and (D // n) % 16 == 0
    z_head = gate_value(head_alpha, head_noise)
    z_unit = gate_value(unit_alpha, unit_noise)
    z_hidden = gate_value(hidden_alpha, hidden_noise)
    z_layer = gate_value(layer_alpha, layer_noise)
    wide = lambda v: jnp.broadcast_to(v[:, None], (v.shape[0], HEAD)).reshape(DH)
    pd = jnp.stack(
        [
            v.astype(f32)
            for v in (
                b_query,
                b_value,
                b_out,
                attention_norm_gain,
                first_shift,
                b_down,
                feedforward_norm_gain,
                second_shift,
                z_hidden,
                hard_hidden,
                wide(z_head),
                wide(hard_heads),
                jnp.broadcast_to(z_layer[0], (DH,)),
                jnp.broadcast_to(z_layer[1], (DH,)),
                jnp.zeros((DH,)),
                jnp.zeros((DH,)),
            )
        ]
    )
    zero = jnp.zeros((FH,), f32)
    pf = jnp.stack([b_up.astype(f32), z_unit, hard_units.astype(f32), zero, zero, zero, zero, zero])
    groups = 4 + 2 * (FH // DH)
    fgroups = FH // DH
    zc = n // 4
    pr = D // n
    hbm = pl.BlockSpec(memory_space=pl.ANY)
    vmem = pl.BlockSpec(memory_space=pltpu.VMEM)
    shape = jax.ShapeDtypeStruct
    out_shape = [
        shape(tokens.shape, bf16),
        shape(tokens.shape, f32),
        shape(tokens.shape, bf16),
        shape((2, M), f32),
        shape((24, DH), f32),
    ]
    out_specs = [hbm, hbm, hbm, vmem, vmem]
    if use_rs:
        out_shape += [shape((4, pr, DH), f32), shape((pr, FH), f32), shape((pr, FH), f32)]
        out_specs += [hbm] * 3
        gshape = (groups, zc, 2, 2, pr, DH)
        r1, r2, r3 = (groups, zc, 2, pr, DH), (groups, zc, pr, DH), (groups, zc - 1, pr, DH)
    else:
        out_shape += [shape((groups, D, DH), bf16)]
        out_specs += [hbm]
        gshape = (groups, D, DH)
        r1 = r2 = r3 = (1, 16, 128)
    dma = pltpu.SemaphoreType.DMA
    V = pltpu.VMEM
    scratch = [
        V((M, D), bf16),
        V((M, D), bf16),
        V((D, 3 * D), bf16),
        V((D, D), bf16),
        V((D, F), bf16),
        V((F, D), bf16),
        V((16, D), f32),
        V((8, F), f32),
        V((M, 3 * D), bf16),
        V((M, 3 * DH), bf16),
        V((M, M), bf16),
        V((D // HEAD, M, M), bf16),
        V((M, D), bf16),
        V((M, D), bf16),
        V((M, DH), bf16),
        V((M, D), f32),
        V((M, D), bf16),
        V((M, D), f32),
        V((M, F), bf16),
        V((M, FH), bf16),
        V((M, F), bf16),
        V((M, FH), bf16),
        V((M, D), f32),
        V((M, D), bf16),
        V((3, D, 2 * M), bf16),
        V((16 * 8, D), f32),
        V((16, F), f32),
        V((2, 24, DH), f32),
        V((24, DH), f32),
        V((4 + zc, 24, DH), f32),
        V((M, 128), f32),
        V(gshape, bf16),
        V(r1, bf16),
        V(r2, bf16),
        V(r3, bf16),
        dma((13 + groups,)),
        dma((10,)),
        dma((10,)),
        dma((18 + zc,)),
        dma((18 + zc,)),
        dma((groups,)),
        dma((groups,)),
        dma((groups,)),
        dma((groups,)),
        dma((groups, zc - 1)),
        dma((groups, zc - 1)),
        pltpu.SemaphoreType.REGULAR,
    ]
    results = pl.pallas_call(
        functools.partial(layer_kernel, (n, D, F, M, use_rs)),
        out_shape=out_shape,
        in_specs=[hbm, hbm, vmem, vmem] + [hbm] * 8,
        out_specs=out_specs,
        scratch_shapes=scratch,
        compiler_params=pltpu.CompilerParams(
            collective_id=0, has_side_effects=True, vmem_limit_bytes=VMEM_LIMIT
        ),
    )(
        tokens,
        teacher,
        segment_ids,
        valid_rows,
        w_query,
        w_key,
        w_value,
        w_out,
        w_up,
        w_down,
        pd,
        pf,
    )
    layer_out, input_grad, hard_out, err, vec = results[:5]
    if use_rs:
        attn, up, down = results[5:]
        wq_grad, wk_grad, wv_grad = attn[1], attn[2], attn[3]
        wout_grad = attn[0].T
        down_grad = down.T
    else:
        scatter = lambda v, dim: lax.psum_scatter(
            v.astype(f32), "rows", scatter_dimension=dim, tiled=True
        )
        grads = results[5]
        side = lambda a: a.transpose(1, 0, 2).reshape(D, FH)
        down_grad = scatter(side(grads[:fgroups]).T, 1)
        up = scatter(side(grads[fgroups : 2 * fgroups]), 0)
        wout_grad = scatter(grads[2 * fgroups].T, 1)
        wq_grad, wk_grad, wv_grad = (scatter(grads[2 * fgroups + 1 + j], 0) for j in range(3))
        vec = lax.psum(vec, "rows")
    ff = vec[16:].reshape(fgroups, 2, DH)
    b_up_grad = ff[:, 0].reshape(FH)
    unit_grad = ff[:, 1].reshape(FH) * (1.0 - z_unit) / temper
    hidden_grad = vec[S_ZH] * (z_hidden * (1.0 - z_hidden) / temper)
    head_grad = jnp.sum(vec[S_ZHEAD].reshape(-1, HEAD), -1) * (z_head * (1.0 - z_head) / temper)
    layer_sum = jnp.sum(vec[S_ZA : S_ZF + 1], -1)
    layer_grad = layer_sum * jnp.stack([1.0, z_layer[1]]) * (1.0 - z_layer) / temper
    return (
        layer_out,
        input_grad,
        wq_grad,
        vec[S_BQ],
        wk_grad,
        wv_grad,
        vec[S_BV],
        wout_grad,
        vec[S_BO],
        vec[S_G1],
        vec[S_S1],
        up,
        b_up_grad,
        down_grad,
        vec[S_BD],
        vec[S_G2],
        vec[S_S2],
        head_grad,
        unit_grad,
        hidden_grad,
        layer_grad,
        hard_out,
        err.reshape(-1),
    )


VMEM_LIMIT = 64 * 1024 * 1024 - 256 * 1024


def solution(mesh):
    in_specs = (
        P("rows", "hid"),
        P("rows", "hid"),
        P("rows", None),
        P("rows", None),
        P(None, "hid"),
        P("hid"),
        P(None, "hid"),
        P(None, "hid"),
        P("hid"),
        P("hid", None),
        P("hid"),
        P("hid"),
        P("hid"),
        P(None, "hid"),
        P("hid"),
        P("hid", None),
        P("hid"),
        P("hid"),
        P("hid"),
        P("hid"),
        P("hid"),
        P("hid"),
        P("hid"),
        P("hid"),
        P("hid"),
        P(),
        P(),
        P("hid"),
        P("hid"),
        P("hid"),
    )
    out_specs = (
        P("rows", "hid"),
        P("rows", "hid"),
        P("rows", "hid"),
        P("hid"),
        P("rows", "hid"),
        P("rows", "hid"),
        P("hid"),
        P("hid", "rows"),
        P("hid"),
        P("hid"),
        P("hid"),
        P("rows", "hid"),
        P("hid"),
        P("hid", "rows"),
        P("hid"),
        P("hid"),
        P("hid"),
        P("hid"),
        P("hid"),
        P("hid"),
        P(),
        P("rows", "hid"),
        P("rows"),
    )
    return jax.shard_map(
        functools.partial(shards, mesh.shape["rows"]), mesh=mesh, in_specs=in_specs, out_specs=out_specs, check_vma=False)
```

```python
import functools

import jax
import jax.numpy as jnp
from jax import lax
from jax.experimental import pallas as pl
from jax.experimental.pallas import tpu as pltpu
from jax.sharding import PartitionSpec as P

HEAD = 64
f32 = jnp.float32
bf16 = jnp.bfloat16
MESH = pl.DeviceIdType.MESH

temper = 2.0 / 3.0
norm_eps = 1e-12
masked_score = -1e30

PB_Q, PB_K, PB_V, PB_O, PG1, PS1, PB_D, PG2, PS2, PZH, PHH, PZHEAD, PHHEAD, PZA, PZF = range(15)
PGZ1, PSZ1, PGZ2, PSZ2, PHG1, PHS1, PHG2, PHS2 = range(16, 24)
S_BQ, S_BV, S_BO, S_G1, S_S1, S_BD, S_G2, S_S2, S_ZH, S_ZHEAD, S_ZA, S_ZF = range(12)
X_TOK, X_HID, X_DDOWN = range(3)
X_DBR = X_DDOWN


def gate_value(alpha, noise):
    return jax.nn.sigmoid((jnp.log(noise) - jnp.log(1.0 - noise) + alpha) / temper)


def mm(a, b):
    return lax.dot_general(a, b, (((1,), (0,)), ((), ())), preferred_element_type=f32)


def mm_nt(a, b):
    return lax.dot_general(a, b, (((1,), (1,)), ((), ())), preferred_element_type=f32)


def loop(count, body):
    def step(i, carry):
        body(i)
        return carry

    lax.fori_loop(0, count, step, 0)


def al(x, m):
    return pl.multiple_of(x, m)


def params(small, pd, pf, cols, fcols):
    (b_query, b_value, b_out, gain1, shift1, b_down, gain2, shift2) = small[:8]
    hidden_alpha, hidden_noise, hard_hidden = small[8:11]
    b_up, unit_alpha, unit_noise, hard_units = small[11:15]
    head_alpha, head_noise, hard_heads = small[15:18]
    layer_alpha, layer_noise = small[18:20]
    DH = b_query.shape[0]
    FH = b_up.shape[0]

    def row(ref):
        return ref[...].astype(f32).reshape(1, ref.shape[0])

    for k, ref in (
        (PB_Q, b_query),
        (PB_V, b_value),
        (PB_O, b_out),
        (PG1, gain1),
        (PS1, shift1),
        (PB_D, b_down),
        (PG2, gain2),
        (PS2, shift2),
        (PHH, hard_hidden),
    ):
        pd[pl.ds(k, 1), cols] = row(ref)
    pd[pl.ds(PB_K, 1), cols] = jnp.zeros((1, DH), f32)
    pd[pl.ds(PZH, 1), cols] = gate_value(row(hidden_alpha), row(hidden_noise))
    for mask, start in ((PZH, PGZ1), (PHH, PHG1)):
        for k, source in enumerate((PG1, PS1, PG2, PS2)):
            pd[pl.ds(start + k, 1), cols] = pd[pl.ds(source, 1), cols] * pd[pl.ds(mask, 1), cols]
    lane = lax.div(lax.broadcasted_iota(jnp.int32, (1, DH), 1), HEAD)

    def spread(ref):
        wide = jnp.zeros((1, DH), f32)
        for j in range(DH // HEAD):
            wide = jnp.where(lane == j, ref[j].astype(f32), wide)
        return wide

    pd[pl.ds(PZHEAD, 1), cols] = gate_value(spread(head_alpha), spread(head_noise))
    pd[pl.ds(PHHEAD, 1), cols] = spread(hard_heads)
    for k in range(2):
        wide = [jnp.full((1, DH), ref[k], f32) for ref in (layer_alpha, layer_noise)]
        pd[pl.ds(PZA + k, 1), cols] = gate_value(*wide)
    pf[pl.ds(0, 1), fcols] = row(b_up)
    pf[pl.ds(1, 1), fcols] = gate_value(row(unit_alpha), row(unit_noise))
    pf[pl.ds(2, 1), fcols] = row(hard_units)


def layer_kernel(dims, *refs):
    n, D, F, M, use_rs = dims
    DH, FH = D // 2, F // 2
    heads = D // HEAD
    pairs = heads // 2
    groups = 4 + 2 * (FH // DH)
    fgroups = FH // DH
    (
        tok_h,
        tea_h,
        seg_ref,
        valid_ref,
        wq_h,
        wk_h,
        wv_h,
        wout_h,
        wup_h,
        wdown_h,
    ) = refs[:10]
    small = refs[10:30]
    outs = refs[30:36]
    layer_out_h, input_grad_h, hard_out_h, err_out, vec_out, grads_out = outs
    (
        tok,
        tea,
        wqkv,
        wout,
        wup,
        wdown,
        pd,
        pf,
        qkv,
        qkv_peer,
        bias,
        probs,
        ctx,
        mixed,
        mixed_peer,
        resid,
        hbf,
        acc,
        act,
        act_peer,
        gp,
        dup_peer,
        dres,
        dbf,
        xt,
        vd,
        vf,
        pack,
        packr,
        packs,
        errs,
        G,
        recv1,
        recv2,
        recv3,
        lsem,
        ssem,
        rsem,
        xs,
        xr,
        s1,
        r1,
        s2,
        r2,
        s3,
        r3,
        credit,
    ) = refs[36:]

    r = lax.axis_index("rows")
    h = lax.axis_index("hid")
    oh = 1 - h
    peer = (r, oh)
    x = lax.rem(r, 2)
    y = lax.rem(lax.div(r, 2), 2)
    z = lax.div(r, 4)
    zc = n // 4

    def chip(cx, cy, cz):
        return (cz * 4 + cy * 2 + cx, h)

    barrier = pltpu.get_barrier_semaphore()
    partners = [peer]
    if use_rs:
        partners += [chip(1 - x, y, z), chip(x, 1 - y, z), chip(1 - x, 1 - y, z)]
        partners += [chip(x, y, lax.rem(z + d, zc)) for d in range(1, zc)]
    for p in partners:
        pl.semaphore_signal(barrier, inc=1, device_id=p, device_id_type=MESH)
    pl.semaphore_wait(barrier, len(partners))

    cols = pl.ds(al(h * DH, 128), DH)
    ocols = pl.ds(al(oh * DH, 128), DH)
    fcols = pl.ds(al(h * FH, 128), FH)
    ofcols = pl.ds(al(oh * FH, 128), FH)
    mine = pl.ds(al(h * M, 128), M)
    other = pl.ds(al(oh * M, 128), M)
    feeds = [
        (tok_h.at[mine], tok_h.at[other], tok.at[:, cols]),
        (wq_h, wq_h, wqkv.at[:, pl.ds(al(h * DH, 128), DH)]),
        (wk_h, wk_h, wqkv.at[:, pl.ds(al(h * DH + D, 128), DH)]),
        (wv_h, wv_h, wqkv.at[:, pl.ds(al(h * DH + 2 * D, 128), DH)]),
        (wout_h, wout_h, wout.at[cols]),
        (wup_h, wup_h, wup.at[:, fcols]),
        (wdown_h, wdown_h, wdown.at[fcols]),
        (tea_h.at[mine], tea_h.at[other], tea.at[:, cols]),
    ]
    local = []
    remote = []

    def feed(i):
        src, src_other, dst = feeds[i]
        far = pltpu.make_async_remote_copy(
            src_ref=src_other,
            dst_ref=dst,
            send_sem=ssem.at[i],
            recv_sem=rsem.at[i],
            device_id=peer,
            device_id_type=MESH,
        )
        far.start()
        near = pltpu.make_async_copy(src, dst, lsem.at[i])
        near.start()
        local.append(near)
        remote.append(far)

    for i in range(4):
        feed(i)
    params(small, pd, pf, cols, fcols)
    shared = []
    for i, at in ((8, pd.at[:, cols]), (9, pf.at[:, fcols])):
        far = pltpu.make_async_remote_copy(
            src_ref=at,
            dst_ref=at,
            send_sem=ssem.at[i],
            recv_sem=rsem.at[i],
            device_id=peer,
            device_id_type=MESH,
        )
        far.start()
        shared.append(far)
    for i in range(4, 8):
        feed(i)
    remote += shared

    def fed(*which):
        for i in which:
            if i < 8:
                local[i].wait()
            remote[i].wait_recv()

    def to_peer(k, src, dst):
        copy = pltpu.make_async_remote_copy(
            src_ref=src,
            dst_ref=dst,
            send_sem=xs.at[k],
            recv_sem=xr.at[k],
            device_id=peer,
            device_id_type=MESH,
        )
        copy.start()
        return copy

    def far_copy(src, dst, send, recv, device):
        return pltpu.make_async_remote_copy(
            src_ref=src,
            dst_ref=dst,
            send_sem=send,
            recv_sem=recv,
            device_id=device,
            device_id_type=MESH,
        )

    half = zc // 2

    def send1(g, b):
        if b == 0:
            src, to = G.at[g, pl.ds(0, half), :, 1 - x], chip(1 - x, y, z)
        else:
            src, to = G.at[g, pl.ds(half, half), 1 - y], chip(x, 1 - y, z)
        return far_copy(src, recv1.at[g, b], s1.at[g, b], r1.at[g, b], to)

    def send2(g, b):
        zs = pl.ds(b * half, half)
        if b == 0:
            src, to = G.at[g, zs, 1 - y, x], chip(x, 1 - y, z)
        else:
            src, to = G.at[g, zs, y, 1 - x], chip(1 - x, y, z)
        return far_copy(src, recv2.at[g, zs], s2.at[g, b], r2.at[g, b], to)

    def send3(g, d):
        to = lax.rem(z + d, zc)
        return far_copy(
            G.at[g, to, y, x], recv3.at[g, d - 1], s3.at[g, d - 1], r3.at[g, d - 1], chip(x, y, to)
        )

    def stage1(g):
        for b in range(2):
            send1(g, b).wait_recv()

            def body(k, b=b):
                for j in range(2):
                    at = G.at[g, k, j, x] if b == 0 else G.at[g, half + k, y, j]
                    at[...] = (at[...].astype(f32) + recv1[g, b, k, j].astype(f32)).astype(bf16)

            loop(half, body)
            send2(g, b).start()

    def stage2(g):
        for b in range(2):
            send2(g, b).wait_recv()

        def body(k):
            at = G.at[g, k, y, x]
            at[...] = (at[...].astype(f32) + recv2[g, k].astype(f32)).astype(bf16)

        loop(zc, body)
        for d in range(1, zc):
            send3(g, d).start()

    def final(g):
        for d in range(1, zc):
            send3(g, d).wait_recv()
        total = G[g, z, y, x].astype(f32)
        for d in range(1, zc):
            total = total + recv3[g, d - 1].astype(f32)
        return total

    def start1(g):
        if use_rs:
            for b in range(2):
                send1(g, b).start()

    ahead = 3

    def tick(i):
        if not use_rs:
            return
        if i < groups:
            stage1(i)
            if i + ahead < groups:
                start1(i + ahead)
        if 1 <= i <= groups:
            stage2(i - 1)

    RT = 128

    def row_loop(body):
        loop(M // RT, lambda i: body(i, pl.ds(al(i * RT, RT), RT)))

    def add_sum(k, value):
        at = vd.at[pl.ds(8 * k, 8)]
        at[...] = at[...] + jnp.sum(value.reshape(RT // 8, 8, D), axis=0)

    def par(k):
        return pd[pl.ds(k, 1), :]

    def normed(resid_tile):
        mean = jnp.sum(resid_tile, -1, keepdims=True) / D
        var = jnp.sum(resid_tile * resid_tile, -1, keepdims=True) / D - mean * mean
        inv = lax.rsqrt(var + norm_eps)
        return (resid_tile - mean) * inv, inv

    dctx = outb = hbf

    def turned(k, sem, i):
        return far_copy(
            xt.at[k, :, pl.ds(al(i * 128, 128), 128)],
            xt.at[k, :, pl.ds(al(M + i * 128, 128), 128)],
            xs.at[32 + 4 * sem + i],
            xr.at[32 + 4 * sem + i],
            peer,
        )

    def turn(value, k, sem, i):
        xt[k, :, pl.ds(al(i * 128, 128), 128)] = value.T
        turned(k, sem, i).start()

    def turned_in(k, sem):
        for i in range(M // 128):
            turned(k, sem, i).wait_recv()

    def turned_out(k, sem):
        for i in range(M // 128):
            turned(k, sem, i).wait_send()

    NT = 256

    def tiles(count, body):
        loop(count // NT, lambda i: body(pl.ds(al(i * NT, NT), NT)))

    def project_out(gate, gain, shift, keep):
        def body(at):
            acc[:, at] = mm(mixed[...], wout[:, at])

        tiles(D, body)

        def body(i, at):
            value = tok[at, :].astype(f32) + acc[at, :] * gate + par(PB_O)
            resid[at, :] = value
            xh, inv = normed(value)
            hidden = (xh * par(gain) + par(shift)).astype(bf16)
            hbf[at, :] = hidden
            if keep:
                turn(hidden, X_HID, 1, i)

        row_loop(body)

    def up(unit_row, keep):
        def body(at):
            u = mm(hbf[...], wup[:, at]) + pf[pl.ds(0, 1), at]
            u2 = u * u
            half = 0.5 * jnp.tanh(u * (0.7978845608 + (0.7978845608 * 0.044715) * u2)) + 0.5
            act[:, at] = (u * half * pf[pl.ds(unit_row, 1), at]).astype(bf16)
            if keep:
                slope = half + u * (2.0 * half * (1.0 - half)) * (
                    0.7978845608 + (3.0 * 0.7978845608 * 0.044715) * u2
                )
                gp[:, at] = slope.astype(bf16)

        tiles(F, body)

    def down():
        def body(at):
            acc[:, at] = mm(act[...], wdown[:, at])

        tiles(D, body)

    row_seg = seg_ref[pl.ds(h, 1), :].astype(f32)
    row_valid = valid_ref[pl.ds(h, 1), :].astype(f32)
    col_seg = jnp.broadcast_to(row_seg, (128, M)).T[:, :1]
    col_valid = jnp.broadcast_to(row_valid, (128, M)).T
    errs[...] = jnp.zeros_like(errs)
    vd[...] = jnp.zeros_like(vd)
    diagonal = lax.broadcasted_iota(jnp.int32, (M, M), 0) == lax.broadcasted_iota(
        jnp.int32, (M, M), 1
    )
    allowed = ((col_seg == row_seg) & (row_valid > 0)) | diagonal
    bias[...] = jnp.where(allowed, 0.0, masked_score).astype(bf16)
    keep_ref = errs
    keep_ref[...] = col_valid

    def project_in(first):
        def body(part):
            at = pl.ds(al(first, 128), DH)
            wide = pl.ds(al(part * D + first, 128), DH)
            value = mm(tok[...], wqkv[:, wide]) + pd[pl.ds(part, 1), at]
            value = value.astype(bf16).astype(f32) * jnp.where(part == 0, HEAD**-0.5, 1.0)
            qkv[:, wide] = value.astype(bf16)

        loop(3, body)

    local[0].wait()
    remote[0].wait_recv()
    for i in (1, 2, 3):
        local[i].wait()
    project_in(h * DH)
    for i in (1, 2, 3, 8, 9):
        remote[i].wait_recv()
    project_in(oh * DH)

    loop(M // 128, lambda i: turn(tok[pl.ds(al(i * 128, 128), 128), :], X_TOK, 0, i))

    lane = lax.broadcasted_iota(jnp.int32, (1, 2 * HEAD), 1)
    head_mask = [(lane < HEAD).astype(bf16), (lane >= HEAD).astype(bf16)]

    QT = 512

    def attend(i):
        p = lax.div(i, M // QT)
        rows = pl.ds(al(lax.rem(i, M // QT) * QT, QT), QT)
        at = pl.ds(al(p * 128, 128), 128)
        q2 = qkv[rows, at]
        k2 = qkv[:, pl.ds(al(p * 128 + D, 128), 128)]
        v2 = qkv[:, pl.ds(al(p * 128 + 2 * D, 128), 128)]
        total = None
        for b in range(2):
            s = mm_nt(q2 * head_mask[b], k2) + bias[rows, :].astype(f32)
            e = jnp.exp(s - jnp.max(s, -1, keepdims=True))
            w = (e * (1.0 / jnp.sum(e, -1, keepdims=True))).astype(bf16)
            probs[2 * p + b, rows] = w
            part = mm(w, v2 * head_mask[b])
            total = part if total is None else total + part
        ctx[rows, at] = total.astype(bf16)
        mixed[rows, at] = (total * pd[pl.ds(PZHEAD, 1), at]).astype(bf16)

    loop(pairs * (M // QT), attend)
    mixed_copy = to_peer(4, mixed.at[:, ocols], mixed_peer)

    fed(4)
    project_out(par(PZA), PGZ1, PSZ1, True)
    fed(5)
    up(1, True)
    act_copy = to_peer(5, act.at[:, ofcols], act_peer)
    fed(6, 7)
    down()

    def second_norm(i, at):
        xh1, inv1 = normed(resid[at, :])
        hidden = xh1 * par(PGZ1) + par(PSZ1)
        dn = acc[at, :]
        xh, inv = normed(hidden + par(PZF) * dn + par(PB_D))
        fin = xh * par(PGZ2) + par(PSZ2)
        outb[at, :] = fin.astype(bf16)
        d = keep_ref[at, :][:, :1] * (fin - tea[at, :].astype(f32))
        add_sum(S_S2, d)
        add_sum(S_G2, d * xh)
        e = d * par(PGZ2)
        dr = inv * (
            e - jnp.sum(e, -1, keepdims=True) / D - xh * (jnp.sum(e * xh, -1, keepdims=True) / D)
        )
        add_sum(S_BD, dr)
        add_sum(S_ZF, dr * dn)
        dres[at, :] = dr
        down_grad_rows = (dr * par(PZF)).astype(bf16)
        dbf[at, :] = down_grad_rows
        turn(down_grad_rows, X_DDOWN, 2, i)

    row_loop(second_norm)
    out_near = pltpu.make_async_copy(outb.at[:, cols], layer_out_h.at[mine], lsem.at[10])
    out_near.start()
    out_far = to_peer(6, outb.at[:, ocols], layer_out_h.at[mine])

    def dactive_tile(at):
        da = mm_nt(dbf[...], wdown[at, :])
        su = jnp.sum((da * act[:, at].astype(f32)).reshape(M // 8, 8, NT), axis=0)
        vf[pl.ds(8, 8), at] = su
        du = (da * pf[pl.ds(1, 1), at] * gp[:, at].astype(f32)).astype(bf16)
        gp[:, at] = du
        vf[pl.ds(0, 8), at] = jnp.sum(du.astype(f32).reshape(M // 8, 8, NT), axis=0)

    early = F // NT // 3
    loop(early, lambda i: dactive_tile(pl.ds(al(i * NT, NT), NT)))

    GT = D // zc if use_rs else D // 4

    def store_grad(g, i, value):
        if use_rs:
            G[g, i] = value.astype(bf16).reshape(2, 2, D // n, DH)
        else:
            G[g, pl.ds(al(i * GT, GT), GT)] = value.astype(bf16)

    def grad_group(g, k, own, far):
        def body(i):
            at = pl.ds(al(i * GT, GT), GT)
            value = mm(xt[k, at, pl.ds(0, M)], own()) + mm(xt[k, at, pl.ds(M, M)], far())
            for b in range(value.shape[1] // DH):
                store_grad(g + b, i, value[:, b * DH : (b + 1) * DH])

        loop(D // GT, body)

    turned_in(X_DDOWN, 2)
    act_copy.wait_recv()

    def down_grad(i):
        grad_group(
            2 * i,
            X_DDOWN,
            lambda: act[:, pl.ds(al(h * FH + i * D, 128), D)],
            lambda: act_peer[:, pl.ds(al(i * D, 128), D)],
        )

    down_grad(0)
    start1(0)
    start1(1)
    down_grad(1)
    start1(2)
    pl.semaphore_signal(credit, inc=1, device_id=peer, device_id_type=MESH)

    loop(F // NT - early, lambda i: dactive_tile(pl.ds(al((i + early) * NT, NT), NT)))
    dup_copy = to_peer(7, gp.at[:, ofcols], dup_peer)

    def dhidden_tile(at):
        acc[:, at] = mm_nt(gp[...], wup[at, :])

    tiles(D, dhidden_tile)
    tick(0)

    turned_in(X_HID, 1)
    dup_copy.wait_recv()

    def up_grad(i):
        grad_group(
            fgroups + 2 * i,
            X_HID,
            lambda: gp[:, pl.ds(al(h * FH + i * D, 128), D)],
            lambda: dup_peer[:, pl.ds(al(i * D, 128), D)],
        )

    loop(fgroups // 2, up_grad)

    out_near.wait()
    out_far.wait_send()
    turned_out(X_DDOWN, 2)
    pl.semaphore_wait(credit, 1)

    def first_norm_back(i, at):
        value = resid[at, :]
        xh, inv = normed(value)
        dh = dres[at, :] + acc[at, :]
        add_sum(S_S1, dh)
        add_sum(S_G1, dh * xh)
        e = dh * par(PGZ1)
        dr = inv * (
            e - jnp.sum(e, -1, keepdims=True) / D - xh * (jnp.sum(e * xh, -1, keepdims=True) / D)
        )
        add_sum(S_BO, dr)
        add_sum(S_ZA, dr * (value - tok[at, :].astype(f32) - par(PB_O)))
        dres[at, :] = dr
        branch_grad = (dr * par(PZA)).astype(bf16)
        dbf[at, :] = branch_grad
        turn(branch_grad, X_DBR, 3, i)

    tick(1)
    row_loop(first_norm_back)
    def dmixed_tile(at):
        dm = mm_nt(dbf[...], wout[at, :])
        vd[pl.ds(8 * S_ZHEAD, 8), at] = jnp.sum(
            (dm * ctx[:, at].astype(f32)).reshape(M // 8, 8, NT), axis=0
        )
        dctx[:, at] = (dm * pd[pl.ds(PZHEAD, 1), at]).astype(bf16)

    tiles(D, dmixed_tile)
    turned_in(X_DBR, 3)
    mixed_copy.wait_recv()
    g_out = 2 * fgroups
    grad_group(g_out, X_DBR, lambda: mixed[:, cols], lambda: mixed_peer[...])
    tick(2)

    own_pairs = pairs // 2

    def send_pair(j, t):
        return far_copy(
            qkv.at[:, pl.ds(al(oh * DH + j * 128 + t * D, 128), 128)],
            qkv_peer.at[:, pl.ds(al(j * DH + t * 128, 128), 128)],
            xs.at[20 + 3 * j + t],
            xr.at[20 + 3 * j + t],
            peer,
        )

    scale = HEAD**-0.5

    def attend_back(i):
        j, own = lax.div(i, 2), lax.rem(i, 2)
        p = lax.rem(oh + own, 2) * own_pairs + j
        qa = pl.ds(al(p * 128, 128), 128)
        ka = pl.ds(al(p * 128 + D, 128), 128)
        va = pl.ds(al(p * 128 + 2 * D, 128), 128)
        k2, v2 = qkv[:, ka], qkv[:, va]
        dkt = dvt = None
        parts = []
        for t in range(M // 256):
            rows = pl.ds(t * 256, 256)
            q2, c2 = qkv[rows, qa], dctx[rows, qa]
            dq = None
            for b in range(2):
                m = head_mask[b]
                w = probs[2 * p + b, rows]
                wf = w.astype(f32)
                dp = mm_nt(c2 * m, v2)
                delta = jnp.sum(wf * dp, -1, keepdims=True)
                ds = (wf * (dp - delta)).astype(bf16)
                a = mm(ds, k2 * m)
                bb = mm((q2 * m).T, ds)
                c = mm((c2 * m).T, w)
                dq = a if dq is None else dq + a
                dkt = bb if dkt is None else dkt + bb
                dvt = c if dvt is None else dvt + c
            parts.append((dq * scale).astype(bf16))
        dq = jnp.concatenate(parts, axis=0)
        dk = dkt.astype(bf16).T
        dv = dvt.astype(bf16).T
        qkv[:, qa] = dq
        qkv[:, ka] = dk
        qkv[:, va] = dv
        vd[pl.ds(8 * S_BQ, 8), qa] = jnp.sum(dq.astype(f32).reshape(M // 8, 8, 128), axis=0)
        vd[pl.ds(8 * S_BV, 8), qa] = jnp.sum(dv.astype(f32).reshape(M // 8, 8, 128), axis=0)

        @pl.when(own == 0)
        def _():
            for t in range(3):
                send_pair(j, t).start()

        @pl.when(own == 1)
        def _():
            for t in range(3):
                send_pair(j, t).wait_recv()
            grad_group(
                g_out + 1 + j,
                X_TOK,
                lambda: jnp.concatenate(
                    [qkv[:, pl.ds(al(h * DH + j * 128 + t * D, 128), 128)] for t in range(3)], axis=1
                ),
                lambda: qkv_peer[:, pl.ds(al(j * DH, 128), DH)],
            )

        for at_step, k in ((2, 3), (5, 4)):

            @pl.when(i == at_step)
            def _(k=k):
                tick(k)

    turned_in(X_TOK, 0)
    loop(pairs, attend_back)

    hidden_sum = 0.0
    for shift_row, gain_row, gain, shift in ((S_S1, S_G1, PG1, PS1), (S_S2, S_G2, PG2, PS2)):
        plain, with_xh = vd[pl.ds(8 * shift_row, 8), :], vd[pl.ds(8 * gain_row, 8), :]
        hidden_sum = hidden_sum + par(gain) * with_xh + par(shift) * plain
        vd[pl.ds(8 * shift_row, 8), :] = plain * par(PZH)
        vd[pl.ds(8 * gain_row, 8), :] = with_xh * par(PZH)
    vd[pl.ds(8 * S_ZH, 8), :] = hidden_sum * (par(PZH) * (1.0 - par(PZH)) / temper)
    zhead, za, zu = par(PZHEAD), pd[pl.ds(PZA, 2), :], pf[pl.ds(1, 1), :]
    for k, factor in (
        (S_ZHEAD, zhead * (1.0 - zhead) / temper),
        (S_ZA, (1.0 - za[0:1]) / temper),
        (S_ZF, za[1:2] * (1.0 - za[1:2]) / temper),
    ):
        vd[pl.ds(8 * k, 8), :] = vd[pl.ds(8 * k, 8), :] * factor
    vf[pl.ds(8, 8), :] = vf[pl.ds(8, 8), :] * ((1.0 - zu) / temper)
    sums = jnp.sum(vd[...].reshape(16, 8, D), axis=1)
    fsums = jnp.sum(vf[...].reshape(2, 8, F), axis=1)
    fold = sums[S_ZA : S_ZF + 1, :DH] + sums[S_ZA : S_ZF + 1, DH:]
    for c in range(2):
        pack[c, 0:16, :] = sums[:, c * DH : (c + 1) * DH]
        pack[c, S_ZA : S_ZF + 1, :] = fold
        for j in range(fgroups):
            pack[c, 16 + 2 * j : 18 + 2 * j, :] = fsums[:, c * FH + j * DH : c * FH + (j + 1) * DH]
    pack_copy = to_peer(8, pack.at[oh], packr)

    def input_tile(at):
        acc[:, at] = dres[:, at] + mm_nt(qkv[...], wqkv[at, :])

    tiles(D, input_tile)
    in_near = pltpu.make_async_copy(acc.at[:, cols], input_grad_h.at[mine], lsem.at[11])
    in_near.start()
    in_far = far_copy(acc.at[:, ocols], input_grad_h.at[mine], xs.at[12], xr.at[12], peer)
    in_far.start()

    pack_copy.wait_recv()
    packs[0] = pack[h] + packr[...]
    plane = []
    if use_rs:
        for k, (cx, cy) in enumerate(((1 - x, y), (x, 1 - y), (1 - x, 1 - y))):
            copy = far_copy(packs.at[0], packs.at[1 + k], xs.at[13 + k], xr.at[13 + k], chip(cx, cy, z))
            copy.start()
            plane.append(copy)
    tick(5)

    in_near.wait()
    in_far.wait_send()
    mixed_copy.wait_send()
    mixed[...] = (ctx[...].astype(f32) * par(PHHEAD)).astype(bf16)
    project_out(1.0, PHG1, PHS1, False)
    act_copy.wait_send()
    tick(6)
    zsum = []
    if use_rs:
        for copy in plane:
            copy.wait_recv()
        packs[4] = (packs[0] + packs[1]) + (packs[2] + packs[3])
        for d in range(1, zc):
            to = lax.rem(z + d, zc)
            copy = far_copy(
                packs.at[4], packs.at[4 + d], xs.at[47 + d], xr.at[47 + d], chip(x, y, to)
            )
            copy.start()
            zsum.append(copy)
    up(2, False)
    tick(7)
    down()
    tick(8)

    def hard_norm(i, at):
        xh1, inv1 = normed(resid[at, :])
        hidden = xh1 * par(PHG1) + par(PHS1)
        xh, inv = normed(hidden + acc[at, :] + par(PB_D))
        fin = xh * par(PHG2) + par(PHS2)
        outb[at, :] = fin.astype(bf16)
        diff = fin - tea[at, :].astype(f32)
        err = jnp.sum(diff * diff, -1, keepdims=True) / D
        keep_ref[at, :] = jnp.broadcast_to(err, (RT, 128))

    row_loop(hard_norm)
    hard_near = pltpu.make_async_copy(outb.at[:, cols], hard_out_h.at[mine], lsem.at[12])
    hard_near.start()
    hard_far = far_copy(outb.at[:, ocols], hard_out_h.at[mine], xs.at[16], xr.at[16], peer)
    hard_far.start()
    pack_copy.wait_send()
    recv_err = vf.at[pl.ds(0, 8), pl.ds(0, M)]
    send_err = vf.at[pl.ds(8, 8), pl.ds(0, M)]
    send_err[...] = errs[...].T[0:8, :]
    err_copy = far_copy(send_err, recv_err, xs.at[17], xr.at[17], peer)
    err_copy.start()

    for i in range(9, groups + 1):
        tick(i)
    if use_rs:
        pr = D // n
        grads = []
        for g in range(groups):
            at = acc.at[pl.ds((g // 2) * pr, pr), pl.ds((g % 2) * DH, DH)]
            at[...] = final(g)
            copy = pltpu.make_async_copy(at, grads_out.at[g], lsem.at[13 + g])
            copy.start()
            grads.append(copy)
        for copy in zsum:
            copy.wait_recv()
        total = packs[4]
        for d in range(1, zc):
            total = total + packs[4 + d]
        vec_out[...] = total
    else:
        vec_out[...] = packs[0]
        grads_near = pltpu.make_async_copy(G, grads_out, lsem.at[13])
        grads_near.start()
        grads_near.wait()
    err_copy.wait_recv()
    err_out[pl.ds(h, 1), :] = send_err[0:1, :]
    err_out[pl.ds(oh, 1), :] = recv_err[0:1, :]

    hard_near.wait()
    hard_far.wait()
    in_far.wait_recv()
    out_far.wait_recv()
    err_copy.wait_send()
    for copy in remote:
        copy.wait_send()
    turned_out(X_TOK, 0)
    turned_out(X_HID, 1)
    turned_out(X_DBR, 3)
    dup_copy.wait_send()
    for j in range(own_pairs):
        for t in range(3):
            send_pair(j, t).wait_send()
    if use_rs:
        for copy in grads:
            copy.wait()
        for copy in plane + zsum:
            copy.wait_send()
        for g in range(groups):
            for b in range(2):
                send1(g, b).wait_send()
                send2(g, b).wait_send()
            for d in range(1, zc):
                send3(g, d).wait_send()


def shards(rows, *args):
    (
        tokens,
        teacher,
        segment_ids,
        valid_rows,
        w_query,
        b_query,
        w_key,
        w_value,
        b_value,
        w_out,
        b_out,
        attention_norm_gain,
        first_shift,
        w_up,
        b_up,
        w_down,
        b_down,
        feedforward_norm_gain,
        second_shift,
        head_alpha,
        head_noise,
        unit_alpha,
        unit_noise,
        hidden_alpha,
        hidden_noise,
        layer_alpha,
        layer_noise,
        hard_heads,
        hard_units,
        hard_hidden,
    ) = args
    DH = tokens.shape[1]
    D = w_query.shape[0]
    FH = w_up.shape[1]
    F = 2 * FH
    blocks, M = segment_ids.shape
    n = rows
    use_rs = n % 8 == 0 and D % n == 0 and (D // n) % 16 == 0
    groups = 4 + 2 * (FH // DH)
    fgroups = FH // DH
    zc = n // 4
    pr = D // n
    hbm = pl.BlockSpec(memory_space=pl.ANY)
    vmem = pl.BlockSpec(memory_space=pltpu.VMEM)
    smem = pl.BlockSpec(memory_space=pltpu.SMEM)
    shape = jax.ShapeDtypeStruct
    out_shape = [
        shape(tokens.shape, bf16),
        shape(tokens.shape, f32),
        shape(tokens.shape, bf16),
        shape((2, M), f32),
        shape((24, DH), f32),
    ]
    out_specs = [hbm, hbm, hbm, vmem, vmem, hbm]
    if use_rs:
        out_shape += [shape((groups, pr, DH), f32)]
        gshape = (groups, zc, 2, 2, pr, DH)
        r1, r2, r3 = (groups, 2, zc // 2, 2, pr, DH), (groups, zc, pr, DH), (groups, zc - 1, pr, DH)
    else:
        out_shape += [shape((groups, D, DH), bf16)]
        gshape = (groups, D, DH)
        r1 = r2 = r3 = (1, 16, 128)
    dma = pltpu.SemaphoreType.DMA
    V = pltpu.VMEM
    scratch = [
        V((M, D), bf16),
        V((M, D), bf16),
        V((D, 3 * D), bf16),
        V((D, D), bf16),
        V((D, F), bf16),
        V((F, D), bf16),
        V((24, D), f32),
        V((8, F), f32),
        V((M, 3 * D), bf16),
        V((M, 3 * DH), bf16),
        V((M, M), bf16),
        V((D // HEAD, M, M), bf16),
        V((M, D), bf16),
        V((M, D), bf16),
        V((M, DH), bf16),
        V((M, D), f32),
        V((M, D), bf16),
        V((M, D), f32),
        V((M, F), bf16),
        V((M, FH), bf16),
        V((M, F), bf16),
        V((M, FH), bf16),
        V((M, D), f32),
        V((M, D), bf16),
        V((3, D, 2 * M), bf16),
        V((16 * 8, D), f32),
        V((16, F), f32),
        V((2, 24, DH), f32),
        V((24, DH), f32),
        V((4 + zc, 24, DH), f32),
        V((M, 128), f32),
        V(gshape, bf16),
        V(r1, bf16),
        V(r2, bf16),
        V(r3, bf16),
        dma((13 + groups,)),
        dma((10,)),
        dma((10,)),
        dma((48 + zc,)),
        dma((48 + zc,)),
        dma((groups, 2)),
        dma((groups, 2)),
        dma((groups, 2)),
        dma((groups, 2)),
        dma((groups, zc - 1)),
        dma((groups, zc - 1)),
        pltpu.SemaphoreType.REGULAR,
    ]
    results = pl.pallas_call(
        functools.partial(layer_kernel, (n, D, F, M, use_rs)),
        out_shape=out_shape,
        in_specs=[hbm, hbm, vmem, vmem] + [hbm] * 6 + [vmem] * 15 + [smem] * 5,
        out_specs=out_specs,
        scratch_shapes=scratch,
        compiler_params=pltpu.CompilerParams(
            collective_id=0, has_side_effects=True, vmem_limit_bytes=VMEM_LIMIT
        ),
    )(
        tokens,
        teacher,
        segment_ids,
        valid_rows,
        w_query,
        w_key,
        w_value,
        w_out,
        w_up,
        w_down,
        b_query,
        b_value,
        b_out,
        attention_norm_gain,
        first_shift,
        b_down,
        feedforward_norm_gain,
        second_shift,
        hidden_alpha,
        hidden_noise,
        hard_hidden,
        b_up,
        unit_alpha,
        unit_noise,
        hard_units,
        head_alpha,
        head_noise,
        hard_heads,
        layer_alpha,
        layer_noise,
    )
    layer_out, input_grad, hard_out, err, vec, grads = results
    if not use_rs:
        vec = lax.psum(vec, "rows")
        side = lambda a: a.transpose(1, 0, 2).reshape(D, -1)
        grads = lax.psum_scatter(
            side(grads).astype(f32), "rows", scatter_dimension=0, tiled=True
        )
        grads = grads.reshape(pr, groups, DH).transpose(1, 0, 2)
    small = (DH,)
    wide = (FH,)
    finished = pl.pallas_call(
        functools.partial(finish_kernel, fgroups),
        out_shape=[
            shape(s, d)
            for s, d in (
                (tokens.shape, bf16),
                (tokens.shape, f32),
                ((pr, DH), f32),
                (small, f32),
                ((pr, DH), f32),
                ((pr, DH), f32),
                (small, f32),
                ((pr, DH), f32),
                (small, f32),
                (small, f32),
                (small, f32),
                ((pr, FH), f32),
                (wide, f32),
                ((pr, FH), f32),
                (small, f32),
                (small, f32),
                (small, f32),
                (head_alpha.shape, f32),
                (wide, f32),
                (small, f32),
                (layer_alpha.shape, f32),
                (tokens.shape, bf16),
                ((tokens.shape[0],), f32),
            )
        ],
        in_specs=[hbm, hbm, hbm] + [vmem] * 3,
        out_specs=[hbm, hbm] + [vmem] * 15 + [smem, vmem, vmem, smem, hbm, vmem],
        scratch_shapes=[V(tokens.shape, bf16), V(tokens.shape, f32), V(tokens.shape, bf16)]
        + [dma((3, 4))] * 2,
    )(layer_out, input_grad, hard_out, err, vec, grads)
    finished = list(finished)
    for k in (7, 13):
        finished[k] = finished[k].T
    return tuple(finished)


def finish_kernel(fgroups, *refs):
    layer_in, input_in, hard_in, err, vec, grads = refs[:6]
    (
        layer_out,
        input_grad,
        wq_grad,
        bq_grad,
        wk_grad,
        wv_grad,
        bv_grad,
        wout_grad,
        bo_grad,
        g1_grad,
        s1_grad,
        wup_grad,
        bup_grad,
        wdown_grad,
        bd_grad,
        g2_grad,
        s2_grad,
        head_grad,
        unit_grad,
        hidden_grad,
        layer_grad,
        hard_out,
        hard_err,
    ) = refs[6:29]
    buffers, (in_sem, out_sem) = refs[29:32], refs[32:34]
    ways = []
    for k, (a, b) in enumerate(
        ((input_in, input_grad), (layer_in, layer_out), (hard_in, hard_out))
    ):
        buffer = buffers[(1, 0, 2)[k]]
        size = a.shape[0] // 4
        for c in range(4):
            at = pl.ds(c * size, size)
            ways.append(
                (
                    pltpu.make_async_copy(a.at[at], buffer.at[at], in_sem.at[k, c]),
                    pltpu.make_async_copy(buffer.at[at], b.at[at], out_sem.at[k, c]),
                )
            )
    for near, _ in ways:
        near.start()
    for near, far in ways:
        near.wait()
        far.start()
    DH = bq_grad.shape[0]
    M = err.shape[1]

    def row(k):
        return vec[pl.ds(k, 1), :]

    for k, ref in (
        (S_BQ, bq_grad),
        (S_BV, bv_grad),
        (S_BO, bo_grad),
        (S_G1, g1_grad),
        (S_S1, s1_grad),
        (S_BD, bd_grad),
        (S_G2, g2_grad),
        (S_S2, s2_grad),
        (S_ZH, hidden_grad),
    ):
        ref[...] = row(k).reshape(DH)
    bup_grad[...] = jnp.concatenate([row(16 + 2 * j) for j in range(fgroups)], axis=1).reshape(
        fgroups * DH
    )
    unit_grad[...] = jnp.concatenate([row(17 + 2 * j) for j in range(fgroups)], axis=1).reshape(
        fgroups * DH
    )
    lane = lax.div(lax.broadcasted_iota(jnp.int32, (1, DH), 1), HEAD)
    heads = row(S_ZHEAD)
    for j in range(DH // HEAD):
        head_grad[j] = jnp.sum(jnp.where(lane == j, heads, 0.0))
    layer_grad[0] = jnp.sum(row(S_ZA))
    layer_grad[1] = jnp.sum(row(S_ZF))
    for b in range(2):
        hard_err[pl.ds(b * M, M)] = err[pl.ds(b, 1), :].reshape(M)
    for g in range(fgroups):
        at = pl.ds(g * DH, DH)
        wdown_grad[:, at] = grads[g]
        wup_grad[:, at] = grads[fgroups + g]
    wout_grad[...] = grads[2 * fgroups]
    for j in range(3):
        to = pl.ds(j * 128, 128)
        for t, ref in enumerate((wq_grad, wk_grad, wv_grad)):
            ref[:, to] = grads[2 * fgroups + 1 + j][:, t * 128 : (t + 1) * 128]
    for _, far in ways:
        far.wait()


VMEM_LIMIT = 64 * 1024 * 1024 - 256 * 1024


def solution(mesh):
    in_specs = (
        P("rows", "hid"),
        P("rows", "hid"),
        P("rows", None),
        P("rows", None),
        P(None, "hid"),
        P("hid"),
        P(None, "hid"),
        P(None, "hid"),
        P("hid"),
        P("hid", None),
        P("hid"),
        P("hid"),
        P("hid"),
        P(None, "hid"),
        P("hid"),
        P("hid", None),
        P("hid"),
        P("hid"),
        P("hid"),
        P("hid"),
        P("hid"),
        P("hid"),
        P("hid"),
        P("hid"),
        P("hid"),
        P(),
        P(),
        P("hid"),
        P("hid"),
        P("hid"),
    )
    out_specs = (
        P("rows", "hid"),
        P("rows", "hid"),
        P("rows", "hid"),
        P("hid"),
        P("rows", "hid"),
        P("rows", "hid"),
        P("hid"),
        P("hid", "rows"),
        P("hid"),
        P("hid"),
        P("hid"),
        P("rows", "hid"),
        P("hid"),
        P("hid", "rows"),
        P("hid"),
        P("hid"),
        P("hid"),
        P("hid"),
        P("hid"),
        P("hid"),
        P(),
        P("rows", "hid"),
        P("rows"),
    )
    return jax.shard_map(
        functools.partial(shards, mesh.shape["rows"]), mesh=mesh, in_specs=in_specs, out_specs=out_specs, check_vma=False)
```

```python
import functools

import jax
import jax.numpy as jnp
from jax import lax
from jax.experimental import pallas as pl
from jax.experimental.pallas import tpu as pltpu
from jax.sharding import PartitionSpec as P

HEAD = 64
f32 = jnp.float32
bf16 = jnp.bfloat16
MESH = pl.DeviceIdType.MESH

temper = 2.0 / 3.0
norm_eps = 1e-12
masked_score = -1e30

PB_Q, PB_K, PB_V, PB_O, PG1, PS1, PB_D, PG2, PS2, PZH, PHH, PZHEAD, PHHEAD, PZA, PZF = range(15)
PGZ1, PSZ1, PGZ2, PSZ2, PHG1, PHS1, PHG2, PHS2 = range(16, 24)
S_BQ, S_BV, S_BO, S_G1, S_S1, S_BD, S_G2, S_S2, S_ZH, S_ZHEAD, S_ZA, S_ZF = range(12)
X_HID, X_DDOWN = range(2)
X_TOK, X_DBR = X_HID, X_DDOWN


def gate_value(alpha, noise):
    return jax.nn.sigmoid((jnp.log(noise) - jnp.log(1.0 - noise) + alpha) / temper)


def mm(a, b):
    return lax.dot_general(a, b, (((1,), (0,)), ((), ())), preferred_element_type=f32)


def mm_nt(a, b):
    return lax.dot_general(a, b, (((1,), (1,)), ((), ())), preferred_element_type=f32)


def loop(count, body):
    def step(i, carry):
        body(i)
        return carry

    lax.fori_loop(0, count, step, 0)


def al(x, m):
    return pl.multiple_of(x, m)


def params(small, pd, pf, cols, fcols):
    (b_query, b_value, b_out, gain1, shift1, b_down, gain2, shift2) = small[:8]
    hidden_alpha, hidden_noise, hard_hidden = small[8:11]
    b_up, unit_alpha, unit_noise, hard_units = small[11:15]
    head_alpha, head_noise, hard_heads = small[15:18]
    layer_alpha, layer_noise = small[18:20]
    DH = b_query.shape[0]
    FH = b_up.shape[0]

    def row(ref):
        return ref[...].astype(f32).reshape(1, ref.shape[0])

    for k, ref in (
        (PB_Q, b_query),
        (PB_V, b_value),
        (PB_O, b_out),
        (PG1, gain1),
        (PS1, shift1),
        (PB_D, b_down),
        (PG2, gain2),
        (PS2, shift2),
        (PHH, hard_hidden),
    ):
        pd[pl.ds(k, 1), cols] = row(ref)
    pd[pl.ds(PB_K, 1), cols] = jnp.zeros((1, DH), f32)
    pd[pl.ds(PZH, 1), cols] = gate_value(row(hidden_alpha), row(hidden_noise))
    for mask, start in ((PZH, PGZ1), (PHH, PHG1)):
        for k, source in enumerate((PG1, PS1, PG2, PS2)):
            pd[pl.ds(start + k, 1), cols] = pd[pl.ds(source, 1), cols] * pd[pl.ds(mask, 1), cols]
    lane = lax.div(lax.broadcasted_iota(jnp.int32, (1, DH), 1), HEAD)

    def spread(ref):
        wide = jnp.zeros((1, DH), f32)
        for j in range(DH // HEAD):
            wide = jnp.where(lane == j, ref[j].astype(f32), wide)
        return wide

    pd[pl.ds(PZHEAD, 1), cols] = gate_value(spread(head_alpha), spread(head_noise))
    pd[pl.ds(PHHEAD, 1), cols] = spread(hard_heads)
    for k in range(2):
        wide = [jnp.full((1, DH), ref[k], f32) for ref in (layer_alpha, layer_noise)]
        pd[pl.ds(PZA + k, 1), cols] = gate_value(*wide)
    pf[pl.ds(0, 1), fcols] = row(b_up)
    pf[pl.ds(1, 1), fcols] = gate_value(row(unit_alpha), row(unit_noise))
    pf[pl.ds(2, 1), fcols] = row(hard_units)


def layer_kernel(dims, *refs):
    n, D, F, M, use_rs = dims
    DH, FH = D // 2, F // 2
    heads = D // HEAD
    pairs = heads // 2
    groups = 4 + 2 * (FH // DH)
    fgroups = FH // DH
    (
        tok_h,
        tea_h,
        seg_ref,
        valid_ref,
        wq_h,
        wk_h,
        wv_h,
        wout_h,
        wup_h,
        wdown_h,
    ) = refs[:10]
    small = refs[10:30]
    outs = refs[30:36]
    layer_out_h, input_grad_h, hard_out_h, err_out, vec_out, grads_out = outs
    (
        tok,
        tea,
        wqkv,
        wout,
        wup,
        wdown,
        pd,
        pf,
        qkv,
        qkv_peer,
        bias,
        probs,
        ctx,
        mixed,
        resid,
        hbf,
        acc,
        act,
        act_peer,
        gp,
        dup_peer,
        dres,
        dbf,
        xt,
        vd,
        vf,
        pack,
        packr,
        packs,
        errs,
        G,
        recv1,
        recv2,
        recv3,
        lsem,
        ssem,
        rsem,
        xs,
        xr,
        s1,
        r1,
        s2,
        r2,
        s3,
        r3,
        zr,
        zs,
        zw,
        credit,
    ) = refs[36:]

    r = lax.axis_index("rows")
    h = lax.axis_index("hid")
    oh = 1 - h
    peer = (r, oh)
    x = lax.rem(r, 2)
    y = lax.rem(lax.div(r, 2), 2)
    z = lax.div(r, 4)
    zc = n // 4

    def chip(cx, cy, cz):
        return (cz * 4 + cy * 2 + cx, h)

    barrier = pltpu.get_barrier_semaphore()
    partners = [peer]
    if use_rs:
        partners += [chip(1 - x, y, z), chip(x, 1 - y, z), chip(1 - x, 1 - y, z)]
        partners += [chip(x, y, lax.rem(z + d, zc)) for d in range(1, zc)]
    for p in partners:
        pl.semaphore_signal(barrier, inc=1, device_id=p, device_id_type=MESH)
    pl.semaphore_wait(barrier, len(partners))

    cols = pl.ds(al(h * DH, 128), DH)
    ocols = pl.ds(al(oh * DH, 128), DH)
    fcols = pl.ds(al(h * FH, 128), FH)
    ofcols = pl.ds(al(oh * FH, 128), FH)
    mine = pl.ds(al(h * M, 128), M)
    other = pl.ds(al(oh * M, 128), M)
    feeds = [
        (tok_h.at[mine], tok_h.at[other], tok.at[:, cols]),
        (wq_h, wq_h, wqkv.at[:, pl.ds(al(h * DH, 128), DH)]),
        (wk_h, wk_h, wqkv.at[:, pl.ds(al(h * DH + D, 128), DH)]),
        (wv_h, wv_h, wqkv.at[:, pl.ds(al(h * DH + 2 * D, 128), DH)]),
        (wout_h, wout_h, wout.at[cols]),
        (wup_h, wup_h, wup.at[:, fcols]),
        (wdown_h, wdown_h, wdown.at[fcols]),
        (tea_h.at[mine], tea_h.at[other], tea.at[:, cols]),
    ]
    local = []
    remote = []

    def feed(i):
        src, src_other, dst = feeds[i]
        far = pltpu.make_async_remote_copy(
            src_ref=src_other,
            dst_ref=dst,
            send_sem=ssem.at[i],
            recv_sem=rsem.at[i],
            device_id=peer,
            device_id_type=MESH,
        )
        far.start()
        near = pltpu.make_async_copy(src, dst, lsem.at[i])
        near.start()
        local.append(near)
        remote.append(far)

    for i in range(4):
        feed(i)
    params(small, pd, pf, cols, fcols)
    shared = []
    for i, at in ((8, pd.at[:, cols]), (9, pf.at[:, fcols])):
        far = pltpu.make_async_remote_copy(
            src_ref=at,
            dst_ref=at,
            send_sem=ssem.at[i],
            recv_sem=rsem.at[i],
            device_id=peer,
            device_id_type=MESH,
        )
        far.start()
        shared.append(far)
    for i in range(4, 8):
        feed(i)
    remote += shared

    def fed(*which):
        for i in which:
            if i < 8:
                local[i].wait()
            remote[i].wait_recv()

    def to_peer(k, src, dst):
        copy = pltpu.make_async_remote_copy(
            src_ref=src,
            dst_ref=dst,
            send_sem=xs.at[k],
            recv_sem=xr.at[k],
            device_id=peer,
            device_id_type=MESH,
        )
        copy.start()
        return copy

    def far_copy(src, dst, send, recv, device):
        return pltpu.make_async_remote_copy(
            src_ref=src,
            dst_ref=dst,
            send_sem=send,
            recv_sem=recv,
            device_id=device,
            device_id_type=MESH,
        )

    half = zc // 2

    last = groups - 1
    runs = 1

    def place(v):
        if v < last:
            return v, pl.ds(0, DH)
        return last, pl.ds(0, DH)

    def send1(v, b):
        g, cs = place(v)
        if b == 0:
            src, to = G.at[g, pl.ds(0, half), :, 1 - x, :, cs], chip(1 - x, y, z)
        else:
            src, to = G.at[g, pl.ds(half, half), 1 - y, :, :, cs], chip(x, 1 - y, z)
        dst = recv1.at[g, b, :, :, :, cs]
        return far_copy(src, dst, s1.at[v, b], r1.at[v, b], to)

    def send2(v, b):
        g, cs = place(v)
        at = pl.ds(b * half, half)
        if b == 0:
            src, to = G.at[g, at, 1 - y, x, :, cs], chip(x, 1 - y, z)
        else:
            src, to = G.at[g, at, y, 1 - x, :, cs], chip(1 - x, y, z)
        dst = recv2.at[g, at, :, cs]
        return far_copy(src, dst, s2.at[v, b], r2.at[v, b], to)

    def send3(v, d):
        g, cs = place(v)
        to = lax.rem(z + d, zc)
        src, dst = G.at[g, to, y, x, :, cs], recv3.at[g, d - 1, :, cs]
        return far_copy(src, dst, s3.at[v, d - 1], r3.at[v, d - 1], chip(x, y, to))

    def start1(v):
        if use_rs:
            for b in range(2):
                send1(v, b).start()

    def stage1(v):
        g, cs = place(v)
        for b in range(2):
            send1(v, b).wait_recv()

            def body(k, b=b):
                for j in range(2):
                    at = G.at[g, k, j, x, :, cs] if b == 0 else G.at[g, half + k, y, j, :, cs]
                    got = recv1[g, b, k, j, :, cs]
                    at[...] = (at[...].astype(f32) + got.astype(f32)).astype(bf16)

            loop(half, body)
            send2(v, b).start()

    def stage2(v):
        g, cs = place(v)
        for b in range(2):
            send2(v, b).wait_recv()

        def body(k):
            at = G.at[g, k, y, x, :, cs]
            at[...] = (at[...].astype(f32) + recv2[g, k, :, cs].astype(f32)).astype(bf16)

        loop(zc, body)
        for d in range(1, zc):
            send3(v, d).start()

    def final(g):
        if g in z_first:
            total = G[g, z, y, x].astype(f32)
            for k in range(3):
                plane_copy(g, k).wait_recv()
                total = total + recv2[g, k].astype(f32)
            return total
        for v in range(g, g + runs if g == last else g + 1):
            for d in range(1, zc):
                send3(v, d).wait_recv()
        total = G[g, z, y, x].astype(f32)
        for d in range(1, zc):
            total = total + recv3[g, d - 1].astype(f32)
        return total

    z_first = (fgroups // 2, 2 * fgroups - 1)
    others = [v for v in range(last + runs) if v not in z_first]
    ahead = 3

    def tick(i):
        if not use_rs:
            return
        if i < len(others):
            stage1(others[i])
            if i + ahead < len(others):
                start1(others[i + ahead])
        if 1 <= i <= len(others):
            stage2(others[i - 1])

    end = (z == 0) | (z == 3)
    near_middle = jnp.where(z == 0, 1, 2)
    near_end = jnp.where(z == 1, 0, 3)
    lowest = jnp.where((z == 0) | (z == 1), 1, 0)

    def z_copy(g, k):
        q = z_first.index(g)
        src, slot, to = (
            (G.at[g, pl.ds(lowest, 2)], recv1.at[g], near_middle),
            (G.at[g, near_end], zr.at[q, 0], near_end),
            (G.at[g, 3 - z], zr.at[q, 1], 3 - z),
            (G.at[g, 3 - near_end], zr.at[q, 1], 3 - near_end),
            (G.at[g, lowest + 2], zr.at[q, 0], near_middle),
        )[k]
        return far_copy(src, slot, zs.at[q, k], zw.at[q, k], chip(x, y, to))

    def plane_copy(g, k):
        q = z_first.index(g)
        cx, cy = ((1 - x, y), (x, 1 - y), (1 - x, 1 - y))[k]
        return far_copy(
            G.at[g, z, cy, cx],
            recv2.at[g, k],
            zs.at[q, 5 + k],
            zw.at[q, 5 + k],
            chip(cx, cy, z),
        )

    def z_begin(g):
        if not use_rs:
            return

        @pl.when(end)
        def _():
            z_copy(g, 0).start()
            z_copy(g, 4).start()

        @pl.when(jnp.logical_not(end))
        def _():
            z_copy(g, 1).start()

    def z_middle(g):
        if not use_rs:
            return
        q = z_first.index(g)

        @pl.when(jnp.logical_not(end))
        def _():
            z_copy(g, 0).wait_recv()
            z_copy(g, 4).wait_recv()

            def body(j):
                for k in range(2):
                    for at, got in (
                        (G.at[g, lowest, j, k], recv1[g, 0, j, k]),
                        (G.at[g, lowest + 1, j, k], recv1[g, 1, j, k]),
                        (G.at[g, lowest + 2, j, k], zr[q, 0, j, k]),
                    ):
                        at[...] = (at[...].astype(f32) + got.astype(f32)).astype(bf16)

            loop(2, body)
            z_copy(g, 2).start()
            z_copy(g, 3).start()

    def z_end(g):
        if not use_rs:
            return
        q = z_first.index(g)

        @pl.when(end)
        def _():
            z_copy(g, 1).wait_recv()
            z_copy(g, 3).wait_recv()

            def body(j):
                for k in range(2):
                    at = G.at[g, z, j, k]
                    at[...] = (
                        at[...].astype(f32) + zr[q, 0, j, k].astype(f32) + zr[q, 1, j, k].astype(f32)
                    ).astype(bf16)

            loop(2, body)

        @pl.when(jnp.logical_not(end))
        def _():
            z_copy(g, 2).wait_recv()

            def body(j):
                for k in range(2):
                    at = G.at[g, z, j, k]
                    at[...] = (at[...].astype(f32) + zr[q, 1, j, k].astype(f32)).astype(bf16)

            loop(2, body)

        for k in range(3):
            plane_copy(g, k).start()

    def z_sent(g):
        @pl.when(end)
        def _():
            z_copy(g, 0).wait_send()
            z_copy(g, 4).wait_send()

        @pl.when(jnp.logical_not(end))
        def _():
            for k in range(1, 4):
                z_copy(g, k).wait_send()

        for k in range(3):
            plane_copy(g, k).wait_send()

    RT = 128

    def row_loop(body):
        loop(M // RT, lambda i: body(i, pl.ds(al(i * RT, RT), RT)))

    def add_sum(k, value):
        at = vd.at[pl.ds(8 * k, 8)]
        at[...] = at[...] + jnp.sum(value.reshape(RT // 8, 8, D), axis=0)

    def par(k):
        return pd[pl.ds(k, 1), :]

    def normed(resid_tile):
        mean = jnp.sum(resid_tile, -1, keepdims=True) / D
        var = jnp.sum(resid_tile * resid_tile, -1, keepdims=True) / D - mean * mean
        inv = lax.rsqrt(var + norm_eps)
        return (resid_tile - mean) * inv, inv

    mixed_peer = qkv_peer.at[:, pl.ds(2 * DH, DH)]
    dctx = outb = hbf

    def turned(k, sem, i):
        return far_copy(
            xt.at[k, :, pl.ds(al(i * 128, 128), 128)],
            xt.at[k, :, pl.ds(al(M + i * 128, 128), 128)],
            xs.at[32 + 4 * sem + i],
            xr.at[32 + 4 * sem + i],
            peer,
        )

    def turn(value, k, sem, i):
        xt[k, :, pl.ds(al(i * 128, 128), 128)] = value.T
        turned(k, sem, i).start()

    def turned_in(k, sem):
        for i in range(M // 128):
            turned(k, sem, i).wait_recv()

    def turned_out(k, sem):
        for i in range(M // 128):
            turned(k, sem, i).wait_send()

    NT = 256

    def tiles(count, body):
        loop(count // NT, lambda i: body(pl.ds(al(i * NT, NT), NT)))

    def project_out(gate, gain, shift, keep):
        def body(at):
            acc[:, at] = mm(mixed[...], wout[:, at])

        tiles(D, body)

        def body(i, at):
            value = tok[at, :].astype(f32) + acc[at, :] * gate + par(PB_O)
            resid[at, :] = value
            xh, inv = normed(value)
            hidden = (xh * par(gain) + par(shift)).astype(bf16)
            hbf[at, :] = hidden
            if keep:
                turn(hidden, X_HID, 1, i)

        row_loop(body)

    def up(unit_row, keep):
        def body(at):
            u = mm(hbf[...], wup[:, at]) + pf[pl.ds(0, 1), at]
            u2 = u * u
            t = jnp.tanh(u * (0.7978845608 + (0.7978845608 * 0.044715) * u2))
            act[:, at] = ((u * (0.5 * pf[pl.ds(unit_row, 1), at])) * (1.0 + t)).astype(bf16)
            if keep:
                gp[:, at] = u.astype(bf16)

        tiles(F, body)

    def down():
        def body(at):
            acc[:, at] = mm(act[...], wdown[:, at])

        tiles(D, body)

    row_seg = seg_ref[pl.ds(h, 1), :].astype(f32)
    row_valid = valid_ref[pl.ds(h, 1), :].astype(f32)
    col_seg = jnp.broadcast_to(row_seg, (128, M)).T[:, :1]
    col_valid = jnp.broadcast_to(row_valid, (128, M)).T
    errs[...] = jnp.zeros_like(errs)
    vd[...] = jnp.zeros_like(vd)
    diagonal = lax.broadcasted_iota(jnp.int32, (M, M), 0) == lax.broadcasted_iota(
        jnp.int32, (M, M), 1
    )
    allowed = ((col_seg == row_seg) & (row_valid > 0)) | diagonal
    bias[...] = jnp.where(allowed, 0.0, masked_score).astype(bf16)
    keep_ref = errs
    keep_ref[...] = col_valid

    def project_in(first):
        def body(part):
            at = pl.ds(al(first, 128), DH)
            wide = pl.ds(al(part * D + first, 128), DH)
            value = mm(tok[...], wqkv[:, wide]) + pd[pl.ds(part, 1), at]
            value = value.astype(bf16).astype(f32) * jnp.where(part == 0, HEAD**-0.5, 1.0)
            qkv[:, wide] = value.astype(bf16)

        loop(3, body)

    local[0].wait()
    remote[0].wait_recv()
    for i in (1, 2, 3):
        local[i].wait()
    project_in(h * DH)


    lane = lax.broadcasted_iota(jnp.int32, (1, 2 * HEAD), 1)
    head_mask = [(lane < HEAD).astype(bf16), (lane >= HEAD).astype(bf16)]

    QT = M

    own_pairs = pairs // 2

    def attend(i):
        @pl.when(i == own_pairs)
        def _():
            for k in (1, 2, 3, 8, 9):
                remote[k].wait_recv()
            project_in(oh * DH)

        p = lax.rem(h * own_pairs + i, pairs)
        rows = pl.ds(0, QT)
        at = pl.ds(al(p * 128, 128), 128)
        q2 = qkv[rows, at]
        k2 = qkv[:, pl.ds(al(p * 128 + D, 128), 128)]
        v2 = qkv[:, pl.ds(al(p * 128 + 2 * D, 128), 128)]
        total = None
        inverse = []
        for b in range(2):
            s = mm_nt(q2 * head_mask[b], k2) + bias[rows, :].astype(f32)
            e = jnp.exp(s - jnp.max(s, -1, keepdims=True))
            w = e.astype(bf16)
            probs[2 * p + b, rows] = w
            part = mm(w, v2 * head_mask[b])
            inverse.append(1.0 / jnp.sum(e, -1, keepdims=True))
            total = part if total is None else total + part
        total = total * jnp.where(lane < HEAD, inverse[0], inverse[1])
        keep_ref[rows, :] = jnp.where(
            lane == 2 * p + 1,
            inverse[0],
            jnp.where(lane == 2 * p + 2, inverse[1], keep_ref[rows, :]),
        )
        ctx[rows, at] = total.astype(bf16)
        mixed[rows, at] = (total * pd[pl.ds(PZHEAD, 1), at]).astype(bf16)

    loop(pairs, attend)
    mixed_copy = to_peer(4, mixed.at[:, ocols], mixed_peer)

    fed(4)
    project_out(par(PZA), PGZ1, PSZ1, True)
    fed(5)
    up(1, True)
    act_copy = to_peer(5, act.at[:, ofcols], act_peer)
    fed(6, 7)
    down()

    def second_norm(i, at):
        xh1, inv1 = normed(resid[at, :])
        hidden = xh1 * par(PGZ1) + par(PSZ1)
        dn = acc[at, :]
        xh, inv = normed(hidden + par(PZF) * dn + par(PB_D))
        fin = xh * par(PGZ2) + par(PSZ2)
        outb[at, :] = fin.astype(bf16)
        d = keep_ref[at, :][:, :1] * (fin - tea[at, :].astype(f32))
        add_sum(S_S2, d)
        add_sum(S_G2, d * xh)
        e = d * par(PGZ2)
        dr = inv * (
            e - jnp.sum(e, -1, keepdims=True) / D - xh * (jnp.sum(e * xh, -1, keepdims=True) / D)
        )
        add_sum(S_BD, dr)
        add_sum(S_ZF, dr * dn)
        dres[at, :] = dr
        down_grad_rows = (dr * par(PZF)).astype(bf16)
        dbf[at, :] = down_grad_rows
        turn(down_grad_rows, X_DDOWN, 2, i)

    row_loop(second_norm)
    out_near = pltpu.make_async_copy(outb.at[:, cols], layer_out_h.at[mine], lsem.at[10])
    out_near.start()
    out_far = to_peer(6, outb.at[:, ocols], layer_out_h.at[mine])

    def dactive_tile(at):
        da = mm_nt(dbf[...], wdown[at, :])
        su = jnp.sum((da * act[:, at].astype(f32)).reshape(M // 8, 8, NT), axis=0)
        vf[pl.ds(8, 8), at] = su
        u = gp[:, at].astype(f32)
        u2 = u * u
        t = jnp.tanh(u * (0.7978845608 + (0.7978845608 * 0.044715) * u2))
        slope = (1.0 + t) * (
            1.0 + (u * (1.0 - t)) * (0.7978845608 + (3.0 * 0.7978845608 * 0.044715) * u2)
        )
        du = (da * (0.5 * pf[pl.ds(1, 1), at]) * slope).astype(bf16)
        gp[:, at] = du
        vf[pl.ds(0, 8), at] = jnp.sum(du.astype(f32).reshape(M // 8, 8, NT), axis=0)

    early = F // NT // 3
    loop(early, lambda i: dactive_tile(pl.ds(al(i * NT, NT), NT)))

    GT = D // zc if use_rs else D // 4

    def store_grad(g, i, value):
        if use_rs:
            G[g, i] = value.astype(bf16).reshape(2, 2, D // n, DH)
        else:
            G[g, pl.ds(al(i * GT, GT), GT)] = value.astype(bf16)

    def grad_group(g, k, own, far):
        def body(i):
            at = pl.ds(al(i * GT, GT), GT)
            value = mm(xt[k, at, pl.ds(0, M)], own()) + mm(xt[k, at, pl.ds(M, M)], far())
            for b in range(value.shape[1] // DH):
                store_grad(g + b, i, value[:, b * DH : (b + 1) * DH])

        loop(D // GT, body)

    turned_in(X_DDOWN, 2)
    act_copy.wait_recv()

    def down_grad(i):
        grad_group(
            2 * i,
            X_DDOWN,
            lambda: act[:, pl.ds(al(h * FH + i * D, 128), D)],
            lambda: act_peer[:, pl.ds(al(i * D, 128), D)],
        )

    down_grad(0)
    start1(0)
    start1(1)
    down_grad(1)
    z_begin(2)
    start1(3)
    pl.semaphore_signal(credit.at[0], inc=1, device_id=peer, device_id_type=MESH)

    loop(F // NT - early, lambda i: dactive_tile(pl.ds(al((i + early) * NT, NT), NT)))
    dup_copy = to_peer(7, gp.at[:, ofcols], dup_peer)

    def dhidden_tile(at):
        acc[:, at] = mm_nt(gp[...], wup[at, :])

    tiles(D, dhidden_tile)

    turned_in(X_HID, 1)
    dup_copy.wait_recv()

    def up_grad(i):
        grad_group(
            fgroups + 2 * i,
            X_HID,
            lambda: gp[:, pl.ds(al(h * FH + i * D, 128), D)],
            lambda: dup_peer[:, pl.ds(al(i * D, 128), D)],
        )

    up_grad(0)
    tick(0)
    up_grad(1)
    pl.semaphore_signal(credit.at[1], inc=1, device_id=peer, device_id_type=MESH)

    out_near.wait()
    out_far.wait_send()
    turned_out(X_DDOWN, 2)
    pl.semaphore_wait(credit.at[0], 1)

    def first_norm_back(i, at):
        value = resid[at, :]
        xh, inv = normed(value)
        dh = dres[at, :] + acc[at, :]
        add_sum(S_S1, dh)
        add_sum(S_G1, dh * xh)
        e = dh * par(PGZ1)
        dr = inv * (
            e - jnp.sum(e, -1, keepdims=True) / D - xh * (jnp.sum(e * xh, -1, keepdims=True) / D)
        )
        add_sum(S_BO, dr)
        add_sum(S_ZA, dr * (value - tok[at, :].astype(f32) - par(PB_O)))
        dres[at, :] = dr
        branch_grad = (dr * par(PZA)).astype(bf16)
        dbf[at, :] = branch_grad
        turn(branch_grad, X_DBR, 3, i)

    z_begin(7)
    tick(1)
    row_loop(first_norm_back)
    def dmixed_tile(i):
        at = pl.ds(i * NT, NT)
        dm = mm_nt(dbf[...], wout[at, :])
        vd[pl.ds(8 * S_ZHEAD, 8), at] = jnp.sum(
            (dm * ctx[:, at].astype(f32)).reshape(M // 8, 8, NT), axis=0
        )
        first = 1 + i * (NT // HEAD)
        inverse = jnp.concatenate(
            [
                jnp.where(lane < HEAD, keep_ref[:, k : k + 1], keep_ref[:, k + 1 : k + 2])
                for k in range(first, first + NT // HEAD, 2)
            ],
            axis=1,
        )
        dctx[:, at] = (dm * pd[pl.ds(PZHEAD, 1), at] * inverse).astype(bf16)

    for i in range(D // NT):
        dmixed_tile(i)
    turned_out(X_HID, 1)
    pl.semaphore_wait(credit.at[1], 1)
    loop(M // 128, lambda i: turn(tok[pl.ds(al(i * 128, 128), 128), :], X_TOK, 0, i))
    turned_in(X_DBR, 3)
    mixed_copy.wait_recv()
    g_out = 2 * fgroups
    grad_group(g_out, X_DBR, lambda: mixed[:, cols], lambda: mixed_peer[...])
    tick(2)
    z_middle(2)

    def send_pair(j, t):
        return far_copy(
            qkv.at[:, pl.ds(al(oh * DH + j * 128 + t * D, 128), 128)],
            qkv_peer.at[:, pl.ds(al(j * DH + t * 128, 128), 128)],
            xs.at[20 + 3 * j + t],
            xr.at[20 + 3 * j + t],
            peer,
        )

    scale = HEAD**-0.5

    def attend_back(i):
        j, own = lax.div(i, 2), lax.rem(i, 2)
        p = lax.rem(oh + own, 2) * own_pairs + j
        qa = pl.ds(al(p * 128, 128), 128)
        ka = pl.ds(al(p * 128 + D, 128), 128)
        va = pl.ds(al(p * 128 + 2 * D, 128), 128)
        k2, v2 = qkv[:, ka], qkv[:, va]
        dkt = dvt = None
        parts = []
        for t in range(M // 256):
            rows = pl.ds(t * 256, 256)
            q2, c2 = qkv[rows, qa], dctx[rows, qa]
            dq = None
            shared = c2.astype(f32) * ctx[rows, qa].astype(f32)
            for b in range(2):
                m = head_mask[b]
                w = probs[2 * p + b, rows]
                dp = mm_nt(c2 * m, v2)
                delta = jnp.sum(shared * m.astype(f32), -1, keepdims=True)
                ds = (w.astype(f32) * (dp - delta)).astype(bf16)
                a = mm(ds, k2 * m)
                bb = mm((q2 * m).T, ds)
                c = mm((c2 * m).T, w)
                dq = a if dq is None else dq + a
                dkt = bb if dkt is None else dkt + bb
                dvt = c if dvt is None else dvt + c
            parts.append((dq * scale).astype(bf16))
        dq = jnp.concatenate(parts, axis=0)
        dk = dkt.astype(bf16).T
        dv = dvt.astype(bf16).T
        qkv[:, qa] = dq
        qkv[:, ka] = dk
        qkv[:, va] = dv
        vd[pl.ds(8 * S_BQ, 8), qa] = jnp.sum(dq.astype(f32).reshape(M // 8, 8, 128), axis=0)
        vd[pl.ds(8 * S_BV, 8), qa] = jnp.sum(dv.astype(f32).reshape(M // 8, 8, 128), axis=0)

        @pl.when(own == 0)
        def _():
            for t in range(3):
                send_pair(j, t).start()

        @pl.when(own == 1)
        def _():
            for t in range(3):
                send_pair(j, t).wait_recv()
            grad_group(
                g_out + 1 + j,
                X_TOK,
                lambda: jnp.concatenate(
                    [qkv[:, pl.ds(al(h * DH + j * 128 + t * D, 128), 128)] for t in range(3)], axis=1
                ),
                lambda: qkv_peer[:, pl.ds(al(j * DH, 128), DH)],
            )

        for at_step, k in ((1, 3), (4, 4)):

            @pl.when(i == at_step)
            def _(k=k):
                tick(k)

    turned_in(X_TOK, 0)
    loop(pairs, attend_back)

    hidden_sum = 0.0
    for shift_row, gain_row, gain, shift in ((S_S1, S_G1, PG1, PS1), (S_S2, S_G2, PG2, PS2)):
        plain, with_xh = vd[pl.ds(8 * shift_row, 8), :], vd[pl.ds(8 * gain_row, 8), :]
        hidden_sum = hidden_sum + par(gain) * with_xh + par(shift) * plain
        vd[pl.ds(8 * shift_row, 8), :] = plain * par(PZH)
        vd[pl.ds(8 * gain_row, 8), :] = with_xh * par(PZH)
    vd[pl.ds(8 * S_ZH, 8), :] = hidden_sum * (par(PZH) * (1.0 - par(PZH)) / temper)
    zhead, za, zu = par(PZHEAD), pd[pl.ds(PZA, 2), :], pf[pl.ds(1, 1), :]
    for k, factor in (
        (S_ZHEAD, zhead * (1.0 - zhead) / temper),
        (S_ZA, (1.0 - za[0:1]) / temper),
        (S_ZF, za[1:2] * (1.0 - za[1:2]) / temper),
    ):
        vd[pl.ds(8 * k, 8), :] = vd[pl.ds(8 * k, 8), :] * factor
    vf[pl.ds(8, 8), :] = vf[pl.ds(8, 8), :] * ((1.0 - zu) / temper)
    sums = jnp.sum(vd[...].reshape(16, 8, D), axis=1)
    fsums = jnp.sum(vf[...].reshape(2, 8, F), axis=1)
    fold = sums[S_ZA : S_ZF + 1, :DH] + sums[S_ZA : S_ZF + 1, DH:]
    for c in range(2):
        pack[c, 0:16, :] = sums[:, c * DH : (c + 1) * DH]
        pack[c, S_ZA : S_ZF + 1, :] = fold
        for j in range(fgroups):
            pack[c, 16 + 2 * j : 18 + 2 * j, :] = fsums[:, c * FH + j * DH : c * FH + (j + 1) * DH]
    pack_copy = to_peer(8, pack.at[oh], packr)

    def input_tile(at):
        acc[:, at] = dres[:, at] + mm_nt(qkv[...], wqkv[at, :])

    tiles(D, input_tile)
    in_near = pltpu.make_async_copy(acc.at[:, cols], input_grad_h.at[mine], lsem.at[11])
    in_near.start()
    in_far = far_copy(acc.at[:, ocols], input_grad_h.at[mine], xs.at[12], xr.at[12], peer)
    in_far.start()

    pack_copy.wait_recv()
    packs[0] = pack[h] + packr[...]
    plane = []
    if use_rs:
        for k, (cx, cy) in enumerate(((1 - x, y), (x, 1 - y), (1 - x, 1 - y))):
            copy = far_copy(packs.at[0], packs.at[1 + k], xs.at[13 + k], xr.at[13 + k], chip(cx, cy, z))
            copy.start()
            plane.append(copy)
    tick(5)
    z_end(2)
    z_middle(7)

    in_near.wait()
    in_far.wait_send()
    mixed_copy.wait_send()
    mixed[...] = (ctx[...].astype(f32) * par(PHHEAD)).astype(bf16)
    project_out(1.0, PHG1, PHS1, False)
    act_copy.wait_send()
    zsum = []
    if use_rs:
        for copy in plane:
            copy.wait_recv()
        packs[4] = (packs[0] + packs[1]) + (packs[2] + packs[3])
        for d in range(1, zc):
            to = lax.rem(z + d, zc)
            copy = far_copy(
                packs.at[4], packs.at[4 + d], xs.at[47 + d], xr.at[47 + d], chip(x, y, to)
            )
            copy.start()
            zsum.append(copy)
    up(2, False)
    tick(6)
    down()
    tick(7)
    z_end(7)

    def hard_norm(i, at):
        xh1, inv1 = normed(resid[at, :])
        hidden = xh1 * par(PHG1) + par(PHS1)
        xh, inv = normed(hidden + acc[at, :] + par(PB_D))
        fin = xh * par(PHG2) + par(PHS2)
        outb[at, :] = fin.astype(bf16)
        diff = fin - tea[at, :].astype(f32)
        err = jnp.sum(diff * diff, -1, keepdims=True) / D
        keep_ref[at, :] = jnp.broadcast_to(err, (RT, 128))

    row_loop(hard_norm)
    hard_near = pltpu.make_async_copy(outb.at[:, cols], hard_out_h.at[mine], lsem.at[12])
    hard_near.start()
    hard_far = far_copy(outb.at[:, ocols], hard_out_h.at[mine], xs.at[16], xr.at[16], peer)
    hard_far.start()
    pack_copy.wait_send()
    recv_err = vf.at[pl.ds(0, 8), pl.ds(0, M)]
    send_err = vf.at[pl.ds(8, 8), pl.ds(0, M)]
    send_err[...] = errs[...].T[0:8, :]
    err_copy = far_copy(send_err, recv_err, xs.at[17], xr.at[17], peer)
    err_copy.start()

    grads = []

    def finish(*which):
        if not use_rs:
            return
        for g in which:
            at = acc.at[pl.ds((g // 2) * (D // n), D // n), pl.ds((g % 2) * DH, DH)]
            at[...] = final(g)
            copy = pltpu.make_async_copy(at, grads_out.at[g], lsem.at[13 + g])
            copy.start()
            grads.append(copy)

    if use_rs:
        tick(8)
        for copy in zsum:
            copy.wait_recv()
        total = packs[4]
        for d in range(1, zc):
            total = total + packs[4 + d]
        vec_out[...] = total
        finish(*(v for v in others[:6]))
        tick(9)
        finish(z_first[0], others[6])
        tick(10)
        finish(others[7], z_first[1])
        for i in range(11, len(others) + 1):
            tick(i)
        finish(last - 1, last)
    else:
        vec_out[...] = packs[0]
        grads_near = pltpu.make_async_copy(G, grads_out, lsem.at[13])
        grads_near.start()
        grads_near.wait()
    err_copy.wait_recv()
    err_out[pl.ds(h, 1), :] = send_err[0:1, :]
    err_out[pl.ds(oh, 1), :] = recv_err[0:1, :]

    hard_near.wait()
    hard_far.wait()
    in_far.wait_recv()
    out_far.wait_recv()
    err_copy.wait_send()
    for copy in remote:
        copy.wait_send()
    turned_out(X_TOK, 0)
    turned_out(X_DBR, 3)
    dup_copy.wait_send()
    for j in range(own_pairs):
        for t in range(3):
            send_pair(j, t).wait_send()
    if use_rs:
        for copy in grads:
            copy.wait()
        for copy in plane + zsum:
            copy.wait_send()
        for g in z_first:
            z_sent(g)
        for g in others:
            for b in range(2):
                send1(g, b).wait_send()
                send2(g, b).wait_send()
            for d in range(1, zc):
                send3(g, d).wait_send()


def shards(rows, *args):
    (
        tokens,
        teacher,
        segment_ids,
        valid_rows,
        w_query,
        b_query,
        w_key,
        w_value,
        b_value,
        w_out,
        b_out,
        attention_norm_gain,
        first_shift,
        w_up,
        b_up,
        w_down,
        b_down,
        feedforward_norm_gain,
        second_shift,
        head_alpha,
        head_noise,
        unit_alpha,
        unit_noise,
        hidden_alpha,
        hidden_noise,
        layer_alpha,
        layer_noise,
        hard_heads,
        hard_units,
        hard_hidden,
    ) = args
    DH = tokens.shape[1]
    D = w_query.shape[0]
    FH = w_up.shape[1]
    F = 2 * FH
    blocks, M = segment_ids.shape
    n = rows
    use_rs = n == 16 and D % n == 0 and (D // n) % 16 == 0
    groups = 4 + 2 * (FH // DH)
    fgroups = FH // DH
    zc = n // 4
    pr = D // n
    hbm = pl.BlockSpec(memory_space=pl.ANY)
    vmem = pl.BlockSpec(memory_space=pltpu.VMEM)
    smem = pl.BlockSpec(memory_space=pltpu.SMEM)
    shape = jax.ShapeDtypeStruct
    out_shape = [
        shape(tokens.shape, bf16),
        shape(tokens.shape, f32),
        shape(tokens.shape, bf16),
        shape((2, M), f32),
        shape((24, DH), f32),
    ]
    out_specs = [hbm, hbm, hbm, vmem, vmem, hbm]
    if use_rs:
        out_shape += [shape((groups, pr, DH), f32)]
        gshape = (groups, zc, 2, 2, pr, DH)
        r4 = (2, 2, 2, 2, pr, DH)
        r1, r2, r3 = (groups, 2, zc // 2, 2, pr, DH), (groups, zc, pr, DH), (groups, zc - 1, pr, DH)
    else:
        out_shape += [shape((groups, D, DH), bf16)]
        gshape = (groups, D, DH)
        r1 = r2 = r3 = r4 = (1, 16, 128)
    dma = pltpu.SemaphoreType.DMA
    V = pltpu.VMEM
    scratch = [
        V((M, D), bf16),
        V((M, D), bf16),
        V((D, 3 * D), bf16),
        V((D, D), bf16),
        V((D, F), bf16),
        V((F, D), bf16),
        V((24, D), f32),
        V((8, F), f32),
        V((M, 3 * D), bf16),
        V((M, 3 * DH), bf16),
        V((M, M), bf16),
        V((D // HEAD, M, M), bf16),
        V((M, D), bf16),
        V((M, D), bf16),
        V((M, D), f32),
        V((M, D), bf16),
        V((M, D), f32),
        V((M, F), bf16),
        V((M, FH), bf16),
        V((M, F), bf16),
        V((M, FH), bf16),
        V((M, D), f32),
        V((M, D), bf16),
        V((2, D, 2 * M), bf16),
        V((16 * 8, D), f32),
        V((16, F), f32),
        V((2, 24, DH), f32),
        V((24, DH), f32),
        V((4 + zc, 24, DH), f32),
        V((M, 128), f32),
        V(gshape, bf16),
        V(r1, bf16),
        V(r2, bf16),
        V(r3, bf16),
        dma((13 + groups,)),
        dma((10,)),
        dma((10,)),
        dma((48 + zc,)),
        dma((48 + zc,)),
        dma((groups + DH // 128 - 1, 2)),
        dma((groups + DH // 128 - 1, 2)),
        dma((groups + DH // 128 - 1, 2)),
        dma((groups + DH // 128 - 1, 2)),
        dma((groups + DH // 128 - 1, zc - 1)),
        dma((groups + DH // 128 - 1, zc - 1)),
        V(r4, bf16),
        dma((2, 8)),
        dma((2, 8)),
        pltpu.SemaphoreType.REGULAR((2,)),
    ]
    results = pl.pallas_call(
        functools.partial(layer_kernel, (n, D, F, M, use_rs)),
        out_shape=out_shape,
        in_specs=[hbm, hbm, vmem, vmem] + [hbm] * 6 + [vmem] * 15 + [smem] * 5,
        out_specs=out_specs,
        scratch_shapes=scratch,
        compiler_params=pltpu.CompilerParams(
            collective_id=0, has_side_effects=True, vmem_limit_bytes=VMEM_LIMIT
        ),
    )(
        tokens,
        teacher,
        segment_ids,
        valid_rows,
        w_query,
        w_key,
        w_value,
        w_out,
        w_up,
        w_down,
        b_query,
        b_value,
        b_out,
        attention_norm_gain,
        first_shift,
        b_down,
        feedforward_norm_gain,
        second_shift,
        hidden_alpha,
        hidden_noise,
        hard_hidden,
        b_up,
        unit_alpha,
        unit_noise,
        hard_units,
        head_alpha,
        head_noise,
        hard_heads,
        layer_alpha,
        layer_noise,
    )
    layer_out, input_grad, hard_out, err, vec, grads = results
    if not use_rs:
        vec = lax.psum(vec, "rows")
        side = lambda a: a.transpose(1, 0, 2).reshape(D, -1)
        grads = lax.psum_scatter(
            side(grads).astype(f32), "rows", scatter_dimension=0, tiled=True
        )
        grads = grads.reshape(pr, groups, DH).transpose(1, 0, 2)
    small = (DH,)
    wide = (FH,)
    finished = pl.pallas_call(
        functools.partial(finish_kernel, fgroups),
        out_shape=[
            shape(s, d)
            for s, d in (
                (tokens.shape, bf16),
                (tokens.shape, f32),
                ((pr, DH), f32),
                (small, f32),
                ((pr, DH), f32),
                ((pr, DH), f32),
                (small, f32),
                ((pr, DH), f32),
                (small, f32),
                (small, f32),
                (small, f32),
                ((pr, FH), f32),
                (wide, f32),
                ((pr, FH), f32),
                (small, f32),
                (small, f32),
                (small, f32),
                (head_alpha.shape, f32),
                (wide, f32),
                (small, f32),
                (layer_alpha.shape, f32),
                (tokens.shape, bf16),
                ((tokens.shape[0],), f32),
            )
        ],
        in_specs=[hbm, hbm, hbm] + [vmem] * 3,
        out_specs=[hbm, hbm] + [vmem] * 15 + [smem, vmem, vmem, smem, hbm, vmem],
        scratch_shapes=[V(tokens.shape, bf16), V(tokens.shape, f32), V(tokens.shape, bf16)]
        + [dma((3, 4))] * 2,
    )(layer_out, input_grad, hard_out, err, vec, grads)
    finished = list(finished)
    for k in (7, 13):
        finished[k] = finished[k].T
    return tuple(finished)


def finish_kernel(fgroups, *refs):
    layer_in, input_in, hard_in, err, vec, grads = refs[:6]
    (
        layer_out,
        input_grad,
        wq_grad,
        bq_grad,
        wk_grad,
        wv_grad,
        bv_grad,
        wout_grad,
        bo_grad,
        g1_grad,
        s1_grad,
        wup_grad,
        bup_grad,
        wdown_grad,
        bd_grad,
        g2_grad,
        s2_grad,
        head_grad,
        unit_grad,
        hidden_grad,
        layer_grad,
        hard_out,
        hard_err,
    ) = refs[6:29]
    buffers, (in_sem, out_sem) = refs[29:32], refs[32:34]
    ways = []
    for k, (a, b) in enumerate(
        ((input_in, input_grad), (layer_in, layer_out), (hard_in, hard_out))
    ):
        buffer = buffers[(1, 0, 2)[k]]
        size = a.shape[0] // 4
        for c in range(4):
            at = pl.ds(c * size, size)
            ways.append(
                (
                    pltpu.make_async_copy(a.at[at], buffer.at[at], in_sem.at[k, c]),
                    pltpu.make_async_copy(buffer.at[at], b.at[at], out_sem.at[k, c]),
                )
            )
    for near, _ in ways:
        near.start()
    for near, far in ways:
        near.wait()
        far.start()
    DH = bq_grad.shape[0]
    M = err.shape[1]

    def row(k):
        return vec[pl.ds(k, 1), :]

    for k, ref in (
        (S_BQ, bq_grad),
        (S_BV, bv_grad),
        (S_BO, bo_grad),
        (S_G1, g1_grad),
        (S_S1, s1_grad),
        (S_BD, bd_grad),
        (S_G2, g2_grad),
        (S_S2, s2_grad),
        (S_ZH, hidden_grad),
    ):
        ref[...] = row(k).reshape(DH)
    bup_grad[...] = jnp.concatenate([row(16 + 2 * j) for j in range(fgroups)], axis=1).reshape(
        fgroups * DH
    )
    unit_grad[...] = jnp.concatenate([row(17 + 2 * j) for j in range(fgroups)], axis=1).reshape(
        fgroups * DH
    )
    lane = lax.div(lax.broadcasted_iota(jnp.int32, (1, DH), 1), HEAD)
    heads = row(S_ZHEAD)
    for j in range(DH // HEAD):
        head_grad[j] = jnp.sum(jnp.where(lane == j, heads, 0.0))
    layer_grad[0] = jnp.sum(row(S_ZA))
    layer_grad[1] = jnp.sum(row(S_ZF))
    for b in range(2):
        hard_err[pl.ds(b * M, M)] = err[pl.ds(b, 1), :].reshape(M)
    for g in range(fgroups):
        at = pl.ds(g * DH, DH)
        wdown_grad[:, at] = grads[g]
        wup_grad[:, at] = grads[fgroups + g]
    wout_grad[...] = grads[2 * fgroups]
    for j in range(3):
        to = pl.ds(j * 128, 128)
        for t, ref in enumerate((wq_grad, wk_grad, wv_grad)):
            ref[:, to] = grads[2 * fgroups + 1 + j][:, t * 128 : (t + 1) * 128]
    for _, far in ways:
        far.wait()


VMEM_LIMIT = 64 * 1024 * 1024 - 64 * 1024


def solution(mesh):
    in_specs = (
        P("rows", "hid"),
        P("rows", "hid"),
        P("rows", None),
        P("rows", None),
        P(None, "hid"),
        P("hid"),
        P(None, "hid"),
        P(None, "hid"),
        P("hid"),
        P("hid", None),
        P("hid"),
        P("hid"),
        P("hid"),
        P(None, "hid"),
        P("hid"),
        P("hid", None),
        P("hid"),
        P("hid"),
        P("hid"),
        P("hid"),
        P("hid"),
        P("hid"),
        P("hid"),
        P("hid"),
        P("hid"),
        P(),
        P(),
        P("hid"),
        P("hid"),
        P("hid"),
    )
    out_specs = (
        P("rows", "hid"),
        P("rows", "hid"),
        P("rows", "hid"),
        P("hid"),
        P("rows", "hid"),
        P("rows", "hid"),
        P("hid"),
        P("hid", "rows"),
        P("hid"),
        P("hid"),
        P("hid"),
        P("rows", "hid"),
        P("hid"),
        P("hid", "rows"),
        P("hid"),
        P("hid"),
        P("hid"),
        P("hid"),
        P("hid"),
        P("hid"),
        P(),
        P("rows", "hid"),
        P("rows"),
    )
    return jax.shard_map(
        functools.partial(shards, mesh.shape["rows"]), mesh=mesh, in_specs=in_specs, out_specs=out_specs, check_vma=False)
```

```python
import functools

import jax
import jax.numpy as jnp
from jax import lax
from jax.experimental import pallas as pl
from jax.experimental.pallas import tpu as pltpu
from jax.sharding import PartitionSpec as P

HEAD = 64
f32 = jnp.float32
bf16 = jnp.bfloat16
MESH = pl.DeviceIdType.MESH

temper = 2.0 / 3.0
norm_eps = 1e-12
masked_score = -1e30

PB_Q, PB_K, PB_V, PB_O, PG1, PS1, PB_D, PG2, PS2, PZH, PHH, PZHEAD, PHHEAD, PZA, PZF = range(15)
PGZ1, PSZ1, PGZ2, PSZ2, PHG1, PHS1, PHG2, PHS2 = range(16, 24)
S_BQ, S_BV, S_BO, S_G1, S_S1, S_BD, S_G2, S_S2, S_ZH, S_ZHEAD, S_ZA, S_ZF = range(12)
X_HID, X_DDOWN = range(2)
X_TOK, X_DBR = X_HID, X_DDOWN


def gate_value(alpha, noise):
    return jax.nn.sigmoid((jnp.log(noise) - jnp.log(1.0 - noise) + alpha) / temper)


def mm(a, b):
    return lax.dot_general(a, b, (((1,), (0,)), ((), ())), preferred_element_type=f32)


def mm_nt(a, b):
    return lax.dot_general(a, b, (((1,), (1,)), ((), ())), preferred_element_type=f32)


def loop(count, body):
    def step(i, carry):
        body(i)
        return carry

    lax.fori_loop(0, count, step, 0)


def al(x, m):
    return pl.multiple_of(x, m)


def params(small, pd, pf, cols, fcols):
    (b_query, b_value, b_out, gain1, shift1, b_down, gain2, shift2) = small[:8]
    hidden_alpha, hidden_noise, hard_hidden = small[8:11]
    b_up, unit_alpha, unit_noise, hard_units = small[11:15]
    head_alpha, head_noise, hard_heads = small[15:18]
    layer_alpha, layer_noise = small[18:20]
    DH = b_query.shape[0]
    FH = b_up.shape[0]

    def row(ref):
        return ref[...].astype(f32).reshape(1, ref.shape[0])

    for k, ref in (
        (PB_Q, b_query),
        (PB_V, b_value),
        (PB_O, b_out),
        (PG1, gain1),
        (PS1, shift1),
        (PB_D, b_down),
        (PG2, gain2),
        (PS2, shift2),
        (PHH, hard_hidden),
    ):
        pd[pl.ds(k, 1), cols] = row(ref)
    pd[pl.ds(PB_K, 1), cols] = jnp.zeros((1, DH), f32)
    pd[pl.ds(PZH, 1), cols] = gate_value(row(hidden_alpha), row(hidden_noise))
    for mask, start in ((PZH, PGZ1), (PHH, PHG1)):
        for k, source in enumerate((PG1, PS1, PG2, PS2)):
            pd[pl.ds(start + k, 1), cols] = pd[pl.ds(source, 1), cols] * pd[pl.ds(mask, 1), cols]
    lane = lax.div(lax.broadcasted_iota(jnp.int32, (1, DH), 1), HEAD)

    def spread(ref):
        wide = jnp.zeros((1, DH), f32)
        for j in range(DH // HEAD):
            wide = jnp.where(lane == j, ref[j].astype(f32), wide)
        return wide

    pd[pl.ds(PZHEAD, 1), cols] = gate_value(spread(head_alpha), spread(head_noise))
    pd[pl.ds(PHHEAD, 1), cols] = spread(hard_heads)
    for k in range(2):
        wide = [jnp.full((1, DH), ref[k], f32) for ref in (layer_alpha, layer_noise)]
        pd[pl.ds(PZA + k, 1), cols] = gate_value(*wide)
    pf[pl.ds(0, 1), fcols] = row(b_up)
    pf[pl.ds(1, 1), fcols] = gate_value(row(unit_alpha), row(unit_noise))
    pf[pl.ds(2, 1), fcols] = row(hard_units)


def layer_kernel(dims, *refs):
    n, D, F, M, use_rs = dims
    DH, FH = D // 2, F // 2
    heads = D // HEAD
    pairs = heads // 2
    groups = 4 + 2 * (FH // DH)
    fgroups = FH // DH
    (
        tok_h,
        tea_h,
        seg_ref,
        valid_ref,
        wq_h,
        wk_h,
        wv_h,
        wout_h,
        wup_h,
        wdown_h,
    ) = refs[:10]
    small = refs[10:30]
    outs = refs[30:36]
    layer_out_h, input_grad_h, hard_out_h, err_out, vec_out, grads_out = outs
    (
        tok,
        tea,
        wqkv,
        wout,
        wup,
        wdown,
        pd,
        pf,
        qkv,
        qkv_peer,
        bias,
        probs,
        ctx,
        mixed,
        resid,
        hbf,
        acc,
        act,
        act_peer,
        gp,
        dup_peer,
        dres,
        dbf,
        xt,
        vd,
        vf,
        pack,
        packr,
        packs,
        errs,
        G,
        recv1,
        recv2,
        recv3,
        lsem,
        ssem,
        rsem,
        xs,
        xr,
        s1,
        r1,
        s2,
        r2,
        s3,
        r3,
        zr,
        zs,
        zw,
        credit,
    ) = refs[36:]

    r = lax.axis_index("rows")
    h = lax.axis_index("hid")
    oh = 1 - h
    peer = (r, oh)
    x = lax.rem(r, 2)
    y = lax.rem(lax.div(r, 2), 2)
    z = lax.div(r, 4)
    zc = n // 4

    def chip(cx, cy, cz):
        return (cz * 4 + cy * 2 + cx, h)

    barrier = pltpu.get_barrier_semaphore()
    partners = [peer]
    if use_rs:
        partners += [chip(1 - x, y, z), chip(x, 1 - y, z), chip(1 - x, 1 - y, z)]
        partners += [chip(x, y, lax.rem(z + d, zc)) for d in range(1, zc)]
    for p in partners:
        pl.semaphore_signal(barrier, inc=1, device_id=p, device_id_type=MESH)
    pl.semaphore_wait(barrier, len(partners))

    cols = pl.ds(al(h * DH, 128), DH)
    ocols = pl.ds(al(oh * DH, 128), DH)
    fcols = pl.ds(al(h * FH, 128), FH)
    ofcols = pl.ds(al(oh * FH, 128), FH)
    mine = pl.ds(al(h * M, 128), M)
    other = pl.ds(al(oh * M, 128), M)
    feeds = [
        (tok_h.at[mine], tok_h.at[other], tok.at[:, cols]),
        (wq_h, wq_h, wqkv.at[:, pl.ds(al(h * DH, 128), DH)]),
        (wk_h, wk_h, wqkv.at[:, pl.ds(al(h * DH + D, 128), DH)]),
        (wv_h, wv_h, wqkv.at[:, pl.ds(al(h * DH + 2 * D, 128), DH)]),
        (wout_h, wout_h, wout.at[cols]),
        (wup_h, wup_h, wup.at[:, fcols]),
        (wdown_h, wdown_h, wdown.at[fcols]),
        (tea_h.at[mine], tea_h.at[other], tea.at[:, cols]),
    ]
    local = []
    remote = []

    def feed(i):
        src, src_other, dst = feeds[i]
        far = pltpu.make_async_remote_copy(
            src_ref=src_other,
            dst_ref=dst,
            send_sem=ssem.at[i],
            recv_sem=rsem.at[i],
            device_id=peer,
            device_id_type=MESH,
        )
        far.start()
        near = pltpu.make_async_copy(src, dst, lsem.at[i])
        near.start()
        local.append(near)
        remote.append(far)

    for i in range(4):
        feed(i)
    params(small, pd, pf, cols, fcols)
    shared = []
    for i, at in ((8, pd.at[:, cols]), (9, pf.at[:, fcols])):
        far = pltpu.make_async_remote_copy(
            src_ref=at,
            dst_ref=at,
            send_sem=ssem.at[i],
            recv_sem=rsem.at[i],
            device_id=peer,
            device_id_type=MESH,
        )
        far.start()
        shared.append(far)
    for i in range(4, 8):
        feed(i)
    remote += shared

    def fed(*which):
        for i in which:
            if i < 8:
                local[i].wait()
            remote[i].wait_recv()

    def to_peer(k, src, dst):
        copy = pltpu.make_async_remote_copy(
            src_ref=src,
            dst_ref=dst,
            send_sem=xs.at[k],
            recv_sem=xr.at[k],
            device_id=peer,
            device_id_type=MESH,
        )
        copy.start()
        return copy

    def far_copy(src, dst, send, recv, device):
        return pltpu.make_async_remote_copy(
            src_ref=src,
            dst_ref=dst,
            send_sem=send,
            recv_sem=recv,
            device_id=device,
            device_id_type=MESH,
        )

    half = zc // 2

    last = groups - 1
    runs = 1

    def place(v):
        if v < last:
            return v, pl.ds(0, DH)
        return last, pl.ds(0, DH)

    def send1(v, b):
        g, cs = place(v)
        if b == 0:
            src, to = G.at[g, pl.ds(0, half), :, 1 - x, :, cs], chip(1 - x, y, z)
        else:
            src, to = G.at[g, pl.ds(half, half), 1 - y, :, :, cs], chip(x, 1 - y, z)
        dst = recv1.at[g, b, :, :, :, cs]
        return far_copy(src, dst, s1.at[v, b], r1.at[v, b], to)

    def send2(v, b):
        g, cs = place(v)
        at = pl.ds(b * half, half)
        if b == 0:
            src, to = G.at[g, at, 1 - y, x, :, cs], chip(x, 1 - y, z)
        else:
            src, to = G.at[g, at, y, 1 - x, :, cs], chip(1 - x, y, z)
        dst = recv2.at[g, at, :, cs]
        return far_copy(src, dst, s2.at[v, b], r2.at[v, b], to)

    def send3(v, d):
        g, cs = place(v)
        to = lax.rem(z + d, zc)
        src, dst = G.at[g, to, y, x, :, cs], recv3.at[g, d - 1, :, cs]
        return far_copy(src, dst, s3.at[v, d - 1], r3.at[v, d - 1], chip(x, y, to))

    def start1(v):
        if use_rs:
            for b in range(2):
                send1(v, b).start()

    def stage1(v):
        g, cs = place(v)
        for b in range(2):
            send1(v, b).wait_recv()

            def body(k, b=b):
                for j in range(2):
                    at = G.at[g, k, j, x, :, cs] if b == 0 else G.at[g, half + k, y, j, :, cs]
                    got = recv1[g, b, k, j, :, cs]
                    at[...] = (at[...].astype(f32) + got.astype(f32)).astype(bf16)

            loop(half, body)
            send2(v, b).start()

    def stage2(v):
        g, cs = place(v)
        for b in range(2):
            send2(v, b).wait_recv()

        def body(k):
            at = G.at[g, k, y, x, :, cs]
            at[...] = (at[...].astype(f32) + recv2[g, k, :, cs].astype(f32)).astype(bf16)

        loop(zc, body)
        for d in range(1, zc):
            send3(v, d).start()

    def final(g):
        if g in z_first:
            total = G[g, z, y, x].astype(f32)
            for k in range(3):
                plane_copy(g, k).wait_recv()
                total = total + recv2[g, k].astype(f32)
            return total
        for v in range(g, g + runs if g == last else g + 1):
            for d in range(1, zc):
                send3(v, d).wait_recv()
        total = G[g, z, y, x].astype(f32)
        for d in range(1, zc):
            total = total + recv3[g, d - 1].astype(f32)
        return total

    z_first = (fgroups // 2, 2 * fgroups - 1)
    others = [v for v in range(last + runs) if v not in z_first]
    ahead = 3

    def tick(i):
        if not use_rs:
            return
        if i < len(others):
            stage1(others[i])
            if i + ahead < len(others):
                start1(others[i + ahead])
        if 1 <= i <= len(others):
            stage2(others[i - 1])

    end = (z == 0) | (z == 3)
    near_middle = jnp.where(z == 0, 1, 2)
    near_end = jnp.where(z == 1, 0, 3)
    lowest = jnp.where((z == 0) | (z == 1), 1, 0)

    def z_copy(g, k):
        q = z_first.index(g)
        src, slot, to = (
            (G.at[g, pl.ds(lowest, 2)], recv1.at[g], near_middle),
            (G.at[g, near_end], zr.at[q, 0], near_end),
            (G.at[g, 3 - z], zr.at[q, 1], 3 - z),
            (G.at[g, 3 - near_end], zr.at[q, 1], 3 - near_end),
            (G.at[g, lowest + 2], zr.at[q, 0], near_middle),
        )[k]
        return far_copy(src, slot, zs.at[q, k], zw.at[q, k], chip(x, y, to))

    def plane_copy(g, k):
        q = z_first.index(g)
        cx, cy = ((1 - x, y), (x, 1 - y), (1 - x, 1 - y))[k]
        return far_copy(
            G.at[g, z, cy, cx],
            recv2.at[g, k],
            zs.at[q, 5 + k],
            zw.at[q, 5 + k],
            chip(cx, cy, z),
        )

    def z_begin(g):
        if not use_rs:
            return

        @pl.when(end)
        def _():
            z_copy(g, 0).start()
            z_copy(g, 4).start()

        @pl.when(jnp.logical_not(end))
        def _():
            z_copy(g, 1).start()

    def z_middle(g):
        if not use_rs:
            return
        q = z_first.index(g)

        @pl.when(jnp.logical_not(end))
        def _():
            z_copy(g, 0).wait_recv()
            z_copy(g, 4).wait_recv()

            def body(j):
                for k in range(2):
                    for at, got in (
                        (G.at[g, lowest, j, k], recv1[g, 0, j, k]),
                        (G.at[g, lowest + 1, j, k], recv1[g, 1, j, k]),
                        (G.at[g, lowest + 2, j, k], zr[q, 0, j, k]),
                    ):
                        at[...] = (at[...].astype(f32) + got.astype(f32)).astype(bf16)

            loop(2, body)
            z_copy(g, 2).start()
            z_copy(g, 3).start()

    def z_end(g):
        if not use_rs:
            return
        q = z_first.index(g)

        @pl.when(end)
        def _():
            z_copy(g, 1).wait_recv()
            z_copy(g, 3).wait_recv()

            def body(j):
                for k in range(2):
                    at = G.at[g, z, j, k]
                    at[...] = (
                        at[...].astype(f32) + zr[q, 0, j, k].astype(f32) + zr[q, 1, j, k].astype(f32)
                    ).astype(bf16)

            loop(2, body)

        @pl.when(jnp.logical_not(end))
        def _():
            z_copy(g, 2).wait_recv()

            def body(j):
                for k in range(2):
                    at = G.at[g, z, j, k]
                    at[...] = (at[...].astype(f32) + zr[q, 1, j, k].astype(f32)).astype(bf16)

            loop(2, body)

        for k in range(3):
            plane_copy(g, k).start()

    def z_sent(g):
        @pl.when(end)
        def _():
            z_copy(g, 0).wait_send()
            z_copy(g, 4).wait_send()

        @pl.when(jnp.logical_not(end))
        def _():
            for k in range(1, 4):
                z_copy(g, k).wait_send()

        for k in range(3):
            plane_copy(g, k).wait_send()

    RT = 128

    def row_loop(body):
        for i in range(M // RT):
            body(i, pl.ds(i * RT, RT))

    def add_sum(k, value):
        at = vd.at[pl.ds(8 * k, 8)]
        at[...] = at[...] + jnp.sum(value.reshape(RT // 8, 8, D), axis=0)

    def par(k):
        return pd[pl.ds(k, 1), :]

    def normed(resid_tile):
        mean = jnp.sum(resid_tile, -1, keepdims=True) / D
        var = jnp.sum(resid_tile * resid_tile, -1, keepdims=True) / D - mean * mean
        inv = lax.rsqrt(var + norm_eps)
        return (resid_tile - mean) * inv, inv

    mixed_peer = qkv_peer.at[:, pl.ds(2 * DH, DH)]
    dctx = outb = hbf

    def turned(k, sem, i):
        return far_copy(
            xt.at[k, :, pl.ds(al(i * 128, 128), 128)],
            xt.at[k, :, pl.ds(al(M + i * 128, 128), 128)],
            xs.at[32 + 4 * sem + i],
            xr.at[32 + 4 * sem + i],
            peer,
        )

    def turn(value, k, sem, i):
        xt[k, :, pl.ds(al(i * 128, 128), 128)] = value.T
        turned(k, sem, i).start()

    def turned_in(k, sem):
        for i in range(M // 128):
            turned(k, sem, i).wait_recv()

    def turned_out(k, sem):
        for i in range(M // 128):
            turned(k, sem, i).wait_send()

    NT = 256

    def tiles(count, body):
        if count == D:
            for i in range(count // NT):
                body(pl.ds(i * NT, NT))
        else:
            loop(count // NT, lambda i: body(pl.ds(al(i * NT, NT), NT)))

    def project_out(gate, gain, shift, keep):
        def body(at):
            acc[:, at] = mm(mixed[...], wout[:, at])

        tiles(D, body)

        def body(i, at):
            value = tok[at, :].astype(f32) + acc[at, :] * gate + par(PB_O)
            resid[at, :] = value
            xh, inv = normed(value)
            hidden = (xh * par(gain) + par(shift)).astype(bf16)
            hbf[at, :] = hidden
            if keep:
                turn(hidden, X_HID, 1, i)

        row_loop(body)

    def up(unit_row, keep):
        def body(at):
            u = mm(hbf[...], wup[:, at]) + pf[pl.ds(0, 1), at]
            u2 = u * u
            t = jnp.tanh(u * (0.7978845608 + (0.7978845608 * 0.044715) * u2))
            act[:, at] = ((u * (0.5 * pf[pl.ds(unit_row, 1), at])) * (1.0 + t)).astype(bf16)
            if keep:
                gp[:, at] = u.astype(bf16)

        tiles(F, body)

    def down():
        def body(at):
            acc[:, at] = mm(act[...], wdown[:, at])

        tiles(D, body)

    row_seg = seg_ref[pl.ds(h, 1), :].astype(f32)
    row_valid = valid_ref[pl.ds(h, 1), :].astype(f32)
    col_seg = jnp.broadcast_to(row_seg, (128, M)).T[:, :1]
    col_valid = jnp.broadcast_to(row_valid, (128, M)).T
    errs[...] = jnp.zeros_like(errs)
    vd[...] = jnp.zeros_like(vd)
    diagonal = lax.broadcasted_iota(jnp.int32, (M, M), 0) == lax.broadcasted_iota(
        jnp.int32, (M, M), 1
    )
    allowed = ((col_seg == row_seg) & (row_valid > 0)) | diagonal
    bias[...] = jnp.where(allowed, 0.0, masked_score).astype(bf16)
    keep_ref = errs
    keep_ref[...] = col_valid

    def project_in(first):
        def body(part):
            at = pl.ds(al(first, 128), DH)
            wide = pl.ds(al(part * D + first, 128), DH)
            value = mm(tok[...], wqkv[:, wide]) + pd[pl.ds(part, 1), at]
            value = value.astype(bf16).astype(f32) * jnp.where(part == 0, HEAD**-0.5, 1.0)
            qkv[:, wide] = value.astype(bf16)

        loop(3, body)

    local[0].wait()
    remote[0].wait_recv()
    for i in (1, 2, 3):
        local[i].wait()
    project_in(h * DH)


    lane = lax.broadcasted_iota(jnp.int32, (1, 2 * HEAD), 1)
    head_mask = [(lane < HEAD).astype(bf16), (lane >= HEAD).astype(bf16)]

    QT = M

    own_pairs = pairs // 2

    def attend(i):
        @pl.when(i == own_pairs)
        def _():
            for k in (1, 2, 3, 8, 9):
                remote[k].wait_recv()
            project_in(oh * DH)

        p = lax.rem(h * own_pairs + i, pairs)
        rows = pl.ds(0, QT)
        at = pl.ds(al(p * 128, 128), 128)
        q2 = qkv[rows, at]
        k2 = qkv[:, pl.ds(al(p * 128 + D, 128), 128)]
        v2 = qkv[:, pl.ds(al(p * 128 + 2 * D, 128), 128)]
        total = None
        inverse = []
        for b in range(2):
            s = mm_nt(q2 * head_mask[b], k2) + bias[rows, :].astype(f32)
            e = jnp.exp(s - jnp.max(s, -1, keepdims=True))
            w = e.astype(bf16)
            probs[2 * p + b, rows] = w
            part = mm(w, v2 * head_mask[b])
            inverse.append(1.0 / jnp.sum(e, -1, keepdims=True))
            total = part if total is None else total + part
        total = total * jnp.where(lane < HEAD, inverse[0], inverse[1])
        keep_ref[rows, :] = jnp.where(
            lane == 2 * p + 1,
            inverse[0],
            jnp.where(lane == 2 * p + 2, inverse[1], keep_ref[rows, :]),
        )
        ctx[rows, at] = total.astype(bf16)
        mixed[rows, at] = (total * pd[pl.ds(PZHEAD, 1), at]).astype(bf16)

    loop(pairs, attend)
    mixed_copy = to_peer(4, mixed.at[:, ocols], mixed_peer)

    fed(4)
    project_out(par(PZA), PGZ1, PSZ1, True)
    fed(5)
    up(1, True)
    act_copy = to_peer(5, act.at[:, ofcols], act_peer)
    fed(6, 7)
    down()

    def second_norm(i, at):
        xh1, inv1 = normed(resid[at, :])
        hidden = xh1 * par(PGZ1) + par(PSZ1)
        dn = acc[at, :]
        xh, inv = normed(hidden + par(PZF) * dn + par(PB_D))
        fin = xh * par(PGZ2) + par(PSZ2)
        outb[at, :] = fin.astype(bf16)
        d = keep_ref[at, :][:, :1] * (fin - tea[at, :].astype(f32))
        add_sum(S_S2, d)
        add_sum(S_G2, d * xh)
        e = d * par(PGZ2)
        dr = inv * (
            e - jnp.sum(e, -1, keepdims=True) / D - xh * (jnp.sum(e * xh, -1, keepdims=True) / D)
        )
        add_sum(S_BD, dr)
        add_sum(S_ZF, dr * dn)
        dres[at, :] = dr
        down_grad_rows = (dr * par(PZF)).astype(bf16)
        dbf[at, :] = down_grad_rows
        turn(down_grad_rows, X_DDOWN, 2, i)

    row_loop(second_norm)
    out_near = pltpu.make_async_copy(outb.at[:, cols], layer_out_h.at[mine], lsem.at[10])
    out_near.start()
    out_far = to_peer(6, outb.at[:, ocols], layer_out_h.at[mine])

    def dactive_tile(at):
        da = mm_nt(dbf[...], wdown[at, :])
        su = jnp.sum((da * act[:, at].astype(f32)).reshape(M // 8, 8, NT), axis=0)
        vf[pl.ds(8, 8), at] = su
        u = gp[:, at].astype(f32)
        u2 = u * u
        t = jnp.tanh(u * (0.7978845608 + (0.7978845608 * 0.044715) * u2))
        slope = (1.0 + t) * (
            1.0 + (u * (1.0 - t)) * (0.7978845608 + (3.0 * 0.7978845608 * 0.044715) * u2)
        )
        du = (da * (0.5 * pf[pl.ds(1, 1), at]) * slope).astype(bf16)
        gp[:, at] = du
        vf[pl.ds(0, 8), at] = jnp.sum(du.astype(f32).reshape(M // 8, 8, NT), axis=0)

    early = F // NT // 3
    loop(early, lambda i: dactive_tile(pl.ds(al(i * NT, NT), NT)))

    GT = D // zc if use_rs else D // 4

    def store_grad(g, i, value):
        if use_rs:
            G[g, i] = value.astype(bf16).reshape(2, 2, D // n, DH)
        else:
            G[g, pl.ds(al(i * GT, GT), GT)] = value.astype(bf16)

    def grad_group(g, k, own, far):
        def body(i):
            at = pl.ds(al(i * GT, GT), GT)
            value = mm(xt[k, at, pl.ds(0, M)], own()) + mm(xt[k, at, pl.ds(M, M)], far())
            for b in range(value.shape[1] // DH):
                store_grad(g + b, i, value[:, b * DH : (b + 1) * DH])

        loop(D // GT, body)

    turned_in(X_DDOWN, 2)
    act_copy.wait_recv()

    def down_grad(i):
        grad_group(
            2 * i,
            X_DDOWN,
            lambda: act[:, pl.ds(al(h * FH + i * D, 128), D)],
            lambda: act_peer[:, pl.ds(al(i * D, 128), D)],
        )

    down_grad(0)
    start1(0)
    start1(1)
    down_grad(1)
    z_begin(2)
    start1(3)
    pl.semaphore_signal(credit.at[0], inc=1, device_id=peer, device_id_type=MESH)

    loop(F // NT - early, lambda i: dactive_tile(pl.ds(al((i + early) * NT, NT), NT)))
    dup_copy = to_peer(7, gp.at[:, ofcols], dup_peer)

    def dhidden_tile(at):
        acc[:, at] = mm_nt(gp[...], wup[at, :])

    tiles(D, dhidden_tile)

    turned_in(X_HID, 1)
    dup_copy.wait_recv()

    def up_grad(i):
        grad_group(
            fgroups + 2 * i,
            X_HID,
            lambda: gp[:, pl.ds(al(h * FH + i * D, 128), D)],
            lambda: dup_peer[:, pl.ds(al(i * D, 128), D)],
        )

    up_grad(0)
    tick(0)
    up_grad(1)
    pl.semaphore_signal(credit.at[1], inc=1, device_id=peer, device_id_type=MESH)

    out_near.wait()
    out_far.wait_send()
    turned_out(X_DDOWN, 2)
    pl.semaphore_wait(credit.at[0], 1)

    def first_norm_back(i, at):
        value = resid[at, :]
        xh, inv = normed(value)
        dh = dres[at, :] + acc[at, :]
        add_sum(S_S1, dh)
        add_sum(S_G1, dh * xh)
        e = dh * par(PGZ1)
        dr = inv * (
            e - jnp.sum(e, -1, keepdims=True) / D - xh * (jnp.sum(e * xh, -1, keepdims=True) / D)
        )
        add_sum(S_BO, dr)
        add_sum(S_ZA, dr * (value - tok[at, :].astype(f32) - par(PB_O)))
        dres[at, :] = dr
        branch_grad = (dr * par(PZA)).astype(bf16)
        dbf[at, :] = branch_grad
        turn(branch_grad, X_DBR, 3, i)

    z_begin(7)
    tick(1)
    row_loop(first_norm_back)
    z_middle(2)
    def dmixed_tile(i):
        at = pl.ds(i * NT, NT)
        dm = mm_nt(dbf[...], wout[at, :])
        vd[pl.ds(8 * S_ZHEAD, 8), at] = jnp.sum(
            (dm * ctx[:, at].astype(f32)).reshape(M // 8, 8, NT), axis=0
        )
        first = 1 + i * (NT // HEAD)
        inverse = jnp.concatenate(
            [
                jnp.where(lane < HEAD, keep_ref[:, k : k + 1], keep_ref[:, k + 1 : k + 2])
                for k in range(first, first + NT // HEAD, 2)
            ],
            axis=1,
        )
        dctx[:, at] = (dm * pd[pl.ds(PZHEAD, 1), at] * inverse).astype(bf16)

    for i in range(D // NT):
        dmixed_tile(i)
    turned_out(X_HID, 1)
    pl.semaphore_wait(credit.at[1], 1)
    loop(M // 128, lambda i: turn(tok[pl.ds(al(i * 128, 128), 128), :], X_TOK, 0, i))
    turned_in(X_DBR, 3)
    mixed_copy.wait_recv()
    g_out = 2 * fgroups
    grad_group(g_out, X_DBR, lambda: mixed[:, cols], lambda: mixed_peer[...])
    tick(2)

    def send_pair(j, t):
        return far_copy(
            qkv.at[:, pl.ds(al(oh * DH + j * 128 + t * D, 128), 128)],
            qkv_peer.at[:, pl.ds(al(j * DH + t * 128, 128), 128)],
            xs.at[20 + 3 * j + t],
            xr.at[20 + 3 * j + t],
            peer,
        )

    scale = HEAD**-0.5

    def attend_back(i):
        j, own = lax.div(i, 2), lax.rem(i, 2)
        p = lax.rem(oh + own, 2) * own_pairs + j
        qa = pl.ds(al(p * 128, 128), 128)
        ka = pl.ds(al(p * 128 + D, 128), 128)
        va = pl.ds(al(p * 128 + 2 * D, 128), 128)
        k2, v2 = qkv[:, ka], qkv[:, va]
        dkt = dvt = None
        parts = []
        for t in range(M // 256):
            rows = pl.ds(t * 256, 256)
            q2, c2 = qkv[rows, qa], dctx[rows, qa]
            dq = None
            shared = c2.astype(f32) * ctx[rows, qa].astype(f32)
            for b in range(2):
                m = head_mask[b]
                w = probs[2 * p + b, rows]
                dp = mm_nt(c2 * m, v2)
                delta = jnp.sum(shared * m.astype(f32), -1, keepdims=True)
                ds = (w.astype(f32) * (dp - delta)).astype(bf16)
                a = mm(ds, k2 * m)
                bb = mm((q2 * m).T, ds)
                c = mm((c2 * m).T, w)
                dq = a if dq is None else dq + a
                dkt = bb if dkt is None else dkt + bb
                dvt = c if dvt is None else dvt + c
            parts.append((dq * scale).astype(bf16))
        dq = jnp.concatenate(parts, axis=0)
        dk = dkt.astype(bf16).T
        dv = dvt.astype(bf16).T
        qkv[:, qa] = dq
        qkv[:, ka] = dk
        qkv[:, va] = dv
        vd[pl.ds(8 * S_BQ, 8), qa] = jnp.sum(dq.astype(f32).reshape(M // 8, 8, 128), axis=0)
        vd[pl.ds(8 * S_BV, 8), qa] = jnp.sum(dv.astype(f32).reshape(M // 8, 8, 128), axis=0)

        @pl.when(own == 0)
        def _():
            for t in range(3):
                send_pair(j, t).start()

        @pl.when(own == 1)
        def _():
            for t in range(3):
                send_pair(j, t).wait_recv()
            grad_group(
                g_out + 1 + j,
                X_TOK,
                lambda: jnp.concatenate(
                    [qkv[:, pl.ds(al(h * DH + j * 128 + t * D, 128), 128)] for t in range(3)], axis=1
                ),
                lambda: qkv_peer[:, pl.ds(al(j * DH, 128), DH)],
            )

        for at_step, k in ((1, 3), (4, 4)):

            @pl.when(i == at_step)
            def _(k=k):
                tick(k)

    turned_in(X_TOK, 0)
    loop(pairs, attend_back)
    z_end(2)
    z_middle(7)

    hidden_sum = 0.0
    for shift_row, gain_row, gain, shift in ((S_S1, S_G1, PG1, PS1), (S_S2, S_G2, PG2, PS2)):
        plain, with_xh = vd[pl.ds(8 * shift_row, 8), :], vd[pl.ds(8 * gain_row, 8), :]
        hidden_sum = hidden_sum + par(gain) * with_xh + par(shift) * plain
        vd[pl.ds(8 * shift_row, 8), :] = plain * par(PZH)
        vd[pl.ds(8 * gain_row, 8), :] = with_xh * par(PZH)
    vd[pl.ds(8 * S_ZH, 8), :] = hidden_sum * (par(PZH) * (1.0 - par(PZH)) / temper)
    zhead, za, zu = par(PZHEAD), pd[pl.ds(PZA, 2), :], pf[pl.ds(1, 1), :]
    for k, factor in (
        (S_ZHEAD, zhead * (1.0 - zhead) / temper),
        (S_ZA, (1.0 - za[0:1]) / temper),
        (S_ZF, za[1:2] * (1.0 - za[1:2]) / temper),
    ):
        vd[pl.ds(8 * k, 8), :] = vd[pl.ds(8 * k, 8), :] * factor
    vf[pl.ds(8, 8), :] = vf[pl.ds(8, 8), :] * ((1.0 - zu) / temper)
    sums = jnp.sum(vd[...].reshape(16, 8, D), axis=1)
    fsums = jnp.sum(vf[...].reshape(2, 8, F), axis=1)
    fold = sums[S_ZA : S_ZF + 1, :DH] + sums[S_ZA : S_ZF + 1, DH:]
    for c in range(2):
        pack[c, 0:16, :] = sums[:, c * DH : (c + 1) * DH]
        pack[c, S_ZA : S_ZF + 1, :] = fold
        for j in range(fgroups):
            pack[c, 16 + 2 * j : 18 + 2 * j, :] = fsums[:, c * FH + j * DH : c * FH + (j + 1) * DH]
    pack_copy = to_peer(8, pack.at[oh], packr)

    def input_tile(at):
        acc[:, at] = dres[:, at] + mm_nt(qkv[...], wqkv[at, :])

    tiles(D, input_tile)
    in_near = pltpu.make_async_copy(acc.at[:, cols], input_grad_h.at[mine], lsem.at[11])
    in_near.start()
    in_far = far_copy(acc.at[:, ocols], input_grad_h.at[mine], xs.at[12], xr.at[12], peer)
    in_far.start()

    pack_copy.wait_recv()
    packs[0] = pack[h] + packr[...]
    plane = []
    if use_rs:
        for k, (cx, cy) in enumerate(((1 - x, y), (x, 1 - y), (1 - x, 1 - y))):
            copy = far_copy(packs.at[0], packs.at[1 + k], xs.at[13 + k], xr.at[13 + k], chip(cx, cy, z))
            copy.start()
            plane.append(copy)
    tick(5)

    in_near.wait()
    in_far.wait_send()
    mixed_copy.wait_send()
    mixed[...] = (ctx[...].astype(f32) * par(PHHEAD)).astype(bf16)
    project_out(1.0, PHG1, PHS1, False)
    act_copy.wait_send()
    zsum = []
    if use_rs:
        for copy in plane:
            copy.wait_recv()
        packs[4] = (packs[0] + packs[1]) + (packs[2] + packs[3])
        for d in range(1, zc):
            to = lax.rem(z + d, zc)
            copy = far_copy(
                packs.at[4], packs.at[4 + d], xs.at[47 + d], xr.at[47 + d], chip(x, y, to)
            )
            copy.start()
            zsum.append(copy)
    up(2, False)
    tick(6)
    down()
    tick(7)
    z_end(7)

    def hard_norm(i, at):
        xh1, inv1 = normed(resid[at, :])
        hidden = xh1 * par(PHG1) + par(PHS1)
        xh, inv = normed(hidden + acc[at, :] + par(PB_D))
        fin = xh * par(PHG2) + par(PHS2)
        outb[at, :] = fin.astype(bf16)
        diff = fin - tea[at, :].astype(f32)
        err = jnp.sum(diff * diff, -1, keepdims=True) / D
        keep_ref[at, :] = jnp.broadcast_to(err, (RT, 128))

    row_loop(hard_norm)
    hard_near = pltpu.make_async_copy(outb.at[:, cols], hard_out_h.at[mine], lsem.at[12])
    hard_near.start()
    hard_far = far_copy(outb.at[:, ocols], hard_out_h.at[mine], xs.at[16], xr.at[16], peer)
    hard_far.start()
    pack_copy.wait_send()
    recv_err = vf.at[pl.ds(0, 8), pl.ds(0, M)]
    send_err = vf.at[pl.ds(8, 8), pl.ds(0, M)]
    send_err[...] = errs[...].T[0:8, :]
    err_copy = far_copy(send_err, recv_err, xs.at[17], xr.at[17], peer)
    err_copy.start()

    grads = []

    def finish(*which):
        if not use_rs:
            return
        for g in which:
            at = acc.at[pl.ds((g // 2) * (D // n), D // n), pl.ds((g % 2) * DH, DH)]
            at[...] = final(g)
            copy = pltpu.make_async_copy(at, grads_out.at[g], lsem.at[13 + g])
            copy.start()
            grads.append(copy)

    if use_rs:
        tick(8)
        for copy in zsum:
            copy.wait_recv()
        total = packs[4]
        for d in range(1, zc):
            total = total + packs[4 + d]
        vec_out[...] = total
        finish(*(v for v in others[:6]))
        tick(9)
        finish(z_first[0], others[6])
        tick(10)
        finish(others[7], z_first[1])
        for i in range(11, len(others) + 1):
            tick(i)
        finish(last - 1, last)
    else:
        vec_out[...] = packs[0]
        grads_near = pltpu.make_async_copy(G, grads_out, lsem.at[13])
        grads_near.start()
        grads_near.wait()
    err_copy.wait_recv()
    err_out[pl.ds(h, 1), :] = send_err[0:1, :]
    err_out[pl.ds(oh, 1), :] = recv_err[0:1, :]

    hard_near.wait()
    hard_far.wait()
    in_far.wait_recv()
    out_far.wait_recv()
    err_copy.wait_send()
    for copy in remote:
        copy.wait_send()
    turned_out(X_TOK, 0)
    turned_out(X_DBR, 3)
    dup_copy.wait_send()
    for j in range(own_pairs):
        for t in range(3):
            send_pair(j, t).wait_send()
    if use_rs:
        for copy in grads:
            copy.wait()
        for copy in plane + zsum:
            copy.wait_send()
        for g in z_first:
            z_sent(g)
        for g in others:
            for b in range(2):
                send1(g, b).wait_send()
                send2(g, b).wait_send()
            for d in range(1, zc):
                send3(g, d).wait_send()


def shards(rows, *args):
    (
        tokens,
        teacher,
        segment_ids,
        valid_rows,
        w_query,
        b_query,
        w_key,
        w_value,
        b_value,
        w_out,
        b_out,
        attention_norm_gain,
        first_shift,
        w_up,
        b_up,
        w_down,
        b_down,
        feedforward_norm_gain,
        second_shift,
        head_alpha,
        head_noise,
        unit_alpha,
        unit_noise,
        hidden_alpha,
        hidden_noise,
        layer_alpha,
        layer_noise,
        hard_heads,
        hard_units,
        hard_hidden,
    ) = args
    DH = tokens.shape[1]
    D = w_query.shape[0]
    FH = w_up.shape[1]
    F = 2 * FH
    blocks, M = segment_ids.shape
    n = rows
    use_rs = n == 16 and D % n == 0 and (D // n) % 16 == 0
    groups = 4 + 2 * (FH // DH)
    fgroups = FH // DH
    zc = n // 4
    pr = D // n
    hbm = pl.BlockSpec(memory_space=pl.ANY)
    vmem = pl.BlockSpec(memory_space=pltpu.VMEM)
    smem = pl.BlockSpec(memory_space=pltpu.SMEM)
    shape = jax.ShapeDtypeStruct
    out_shape = [
        shape(tokens.shape, bf16),
        shape(tokens.shape, f32),
        shape(tokens.shape, bf16),
        shape((2, M), f32),
        shape((24, DH), f32),
    ]
    out_specs = [hbm, hbm, hbm, vmem, vmem, hbm]
    if use_rs:
        out_shape += [shape((groups, pr, DH), f32)]
        gshape = (groups, zc, 2, 2, pr, DH)
        r4 = (2, 2, 2, 2, pr, DH)
        r1, r2, r3 = (groups, 2, zc // 2, 2, pr, DH), (groups, zc, pr, DH), (groups, zc - 1, pr, DH)
    else:
        out_shape += [shape((groups, D, DH), bf16)]
        gshape = (groups, D, DH)
        r1 = r2 = r3 = r4 = (1, 16, 128)
    dma = pltpu.SemaphoreType.DMA
    V = pltpu.VMEM
    scratch = [
        V((M, D), bf16),
        V((M, D), bf16),
        V((D, 3 * D), bf16),
        V((D, D), bf16),
        V((D, F), bf16),
        V((F, D), bf16),
        V((24, D), f32),
        V((8, F), f32),
        V((M, 3 * D), bf16),
        V((M, 3 * DH), bf16),
        V((M, M), bf16),
        V((D // HEAD, M, M), bf16),
        V((M, D), bf16),
        V((M, D), bf16),
        V((M, D), f32),
        V((M, D), bf16),
        V((M, D), f32),
        V((M, F), bf16),
        V((M, FH), bf16),
        V((M, F), bf16),
        V((M, FH), bf16),
        V((M, D), f32),
        V((M, D), bf16),
        V((2, D, 2 * M), bf16),
        V((16 * 8, D), f32),
        V((16, F), f32),
        V((2, 24, DH), f32),
        V((24, DH), f32),
        V((4 + zc, 24, DH), f32),
        V((M, 128), f32),
        V(gshape, bf16),
        V(r1, bf16),
        V(r2, bf16),
        V(r3, bf16),
        dma((13 + groups,)),
        dma((10,)),
        dma((10,)),
        dma((48 + zc,)),
        dma((48 + zc,)),
        dma((groups + DH // 128 - 1, 2)),
        dma((groups + DH // 128 - 1, 2)),
        dma((groups + DH // 128 - 1, 2)),
        dma((groups + DH // 128 - 1, 2)),
        dma((groups + DH // 128 - 1, zc - 1)),
        dma((groups + DH // 128 - 1, zc - 1)),
        V(r4, bf16),
        dma((2, 8)),
        dma((2, 8)),
        pltpu.SemaphoreType.REGULAR((2,)),
    ]
    results = pl.pallas_call(
        functools.partial(layer_kernel, (n, D, F, M, use_rs)),
        out_shape=out_shape,
        in_specs=[hbm, hbm, vmem, vmem] + [hbm] * 6 + [vmem] * 15 + [smem] * 5,
        out_specs=out_specs,
        scratch_shapes=scratch,
        compiler_params=pltpu.CompilerParams(
            collective_id=0, has_side_effects=True, vmem_limit_bytes=VMEM_LIMIT
        ),
    )(
        tokens,
        teacher,
        segment_ids,
        valid_rows,
        w_query,
        w_key,
        w_value,
        w_out,
        w_up,
        w_down,
        b_query,
        b_value,
        b_out,
        attention_norm_gain,
        first_shift,
        b_down,
        feedforward_norm_gain,
        second_shift,
        hidden_alpha,
        hidden_noise,
        hard_hidden,
        b_up,
        unit_alpha,
        unit_noise,
        hard_units,
        head_alpha,
        head_noise,
        hard_heads,
        layer_alpha,
        layer_noise,
    )
    layer_out, input_grad, hard_out, err, vec, grads = results
    if not use_rs:
        vec = lax.psum(vec, "rows")
        side = lambda a: a.transpose(1, 0, 2).reshape(D, -1)
        grads = lax.psum_scatter(
            side(grads).astype(f32), "rows", scatter_dimension=0, tiled=True
        )
        grads = grads.reshape(pr, groups, DH).transpose(1, 0, 2)
    small = (DH,)
    wide = (FH,)
    finished = pl.pallas_call(
        functools.partial(finish_kernel, fgroups),
        out_shape=[
            shape(s, d)
            for s, d in (
                (tokens.shape, bf16),
                (tokens.shape, f32),
                ((pr, DH), f32),
                (small, f32),
                ((pr, DH), f32),
                ((pr, DH), f32),
                (small, f32),
                ((pr, DH), f32),
                (small, f32),
                (small, f32),
                (small, f32),
                ((pr, FH), f32),
                (wide, f32),
                ((pr, FH), f32),
                (small, f32),
                (small, f32),
                (small, f32),
                (head_alpha.shape, f32),
                (wide, f32),
                (small, f32),
                (layer_alpha.shape, f32),
                (tokens.shape, bf16),
                ((tokens.shape[0],), f32),
            )
        ],
        in_specs=[hbm, hbm, hbm] + [vmem] * 3,
        out_specs=[hbm, hbm] + [vmem] * 15 + [smem, vmem, vmem, smem, hbm, vmem],
        scratch_shapes=[V(tokens.shape, bf16), V(tokens.shape, f32), V(tokens.shape, bf16)]
        + [dma((3, 4))] * 2,
    )(layer_out, input_grad, hard_out, err, vec, grads)
    finished = list(finished)
    for k in (7, 13):
        finished[k] = finished[k].T
    return tuple(finished)


def finish_kernel(fgroups, *refs):
    layer_in, input_in, hard_in, err, vec, grads = refs[:6]
    (
        layer_out,
        input_grad,
        wq_grad,
        bq_grad,
        wk_grad,
        wv_grad,
        bv_grad,
        wout_grad,
        bo_grad,
        g1_grad,
        s1_grad,
        wup_grad,
        bup_grad,
        wdown_grad,
        bd_grad,
        g2_grad,
        s2_grad,
        head_grad,
        unit_grad,
        hidden_grad,
        layer_grad,
        hard_out,
        hard_err,
    ) = refs[6:29]
    buffers, (in_sem, out_sem) = refs[29:32], refs[32:34]
    ways = []
    for k, (a, b) in enumerate(
        ((input_in, input_grad), (layer_in, layer_out), (hard_in, hard_out))
    ):
        buffer = buffers[(1, 0, 2)[k]]
        size = a.shape[0] // 4
        for c in range(4):
            at = pl.ds(c * size, size)
            ways.append(
                (
                    pltpu.make_async_copy(a.at[at], buffer.at[at], in_sem.at[k, c]),
                    pltpu.make_async_copy(buffer.at[at], b.at[at], out_sem.at[k, c]),
                )
            )
    for near, _ in ways:
        near.start()
    for near, far in ways:
        near.wait()
        far.start()
    DH = bq_grad.shape[0]
    M = err.shape[1]

    def row(k):
        return vec[pl.ds(k, 1), :]

    for k, ref in (
        (S_BQ, bq_grad),
        (S_BV, bv_grad),
        (S_BO, bo_grad),
        (S_G1, g1_grad),
        (S_S1, s1_grad),
        (S_BD, bd_grad),
        (S_G2, g2_grad),
        (S_S2, s2_grad),
        (S_ZH, hidden_grad),
    ):
        ref[...] = row(k).reshape(DH)
    bup_grad[...] = jnp.concatenate([row(16 + 2 * j) for j in range(fgroups)], axis=1).reshape(
        fgroups * DH
    )
    unit_grad[...] = jnp.concatenate([row(17 + 2 * j) for j in range(fgroups)], axis=1).reshape(
        fgroups * DH
    )
    lane = lax.div(lax.broadcasted_iota(jnp.int32, (1, DH), 1), HEAD)
    heads = row(S_ZHEAD)
    for j in range(DH // HEAD):
        head_grad[j] = jnp.sum(jnp.where(lane == j, heads, 0.0))
    layer_grad[0] = jnp.sum(row(S_ZA))
    layer_grad[1] = jnp.sum(row(S_ZF))
    for b in range(2):
        hard_err[pl.ds(b * M, M)] = err[pl.ds(b, 1), :].reshape(M)
    for g in range(fgroups):
        at = pl.ds(g * DH, DH)
        wdown_grad[:, at] = grads[g]
        wup_grad[:, at] = grads[fgroups + g]
    wout_grad[...] = grads[2 * fgroups]
    for j in range(3):
        to = pl.ds(j * 128, 128)
        for t, ref in enumerate((wq_grad, wk_grad, wv_grad)):
            ref[:, to] = grads[2 * fgroups + 1 + j][:, t * 128 : (t + 1) * 128]
    for _, far in ways:
        far.wait()


VMEM_LIMIT = 64 * 1024 * 1024 - 64 * 1024


def solution(mesh):
    in_specs = (
        P("rows", "hid"),
        P("rows", "hid"),
        P("rows", None),
        P("rows", None),
        P(None, "hid"),
        P("hid"),
        P(None, "hid"),
        P(None, "hid"),
        P("hid"),
        P("hid", None),
        P("hid"),
        P("hid"),
        P("hid"),
        P(None, "hid"),
        P("hid"),
        P("hid", None),
        P("hid"),
        P("hid"),
        P("hid"),
        P("hid"),
        P("hid"),
        P("hid"),
        P("hid"),
        P("hid"),
        P("hid"),
        P(),
        P(),
        P("hid"),
        P("hid"),
        P("hid"),
    )
    out_specs = (
        P("rows", "hid"),
        P("rows", "hid"),
        P("rows", "hid"),
        P("hid"),
        P("rows", "hid"),
        P("rows", "hid"),
        P("hid"),
        P("hid", "rows"),
        P("hid"),
        P("hid"),
        P("hid"),
        P("rows", "hid"),
        P("hid"),
        P("hid", "rows"),
        P("hid"),
        P("hid"),
        P("hid"),
        P("hid"),
        P("hid"),
        P("hid"),
        P(),
        P("rows", "hid"),
        P("rows"),
    )
    return jax.shard_map(
        functools.partial(shards, mesh.shape["rows"]), mesh=mesh, in_specs=in_specs, out_specs=out_specs, check_vma=False)
```
